512 devices in a mesh: dp: 128 (over y, z, core), mp: 4 (over x).
Axes of the slice: x: 4, y: 8, z: 8, core: 2. Of those that a mesh axis runs over, the one named last changes fastest.
Arguments:
- stream_map: int32 [128], replicated, may hold values from 0 to 127, each once
- lengths: int32 [128], P('dp'), may hold values from 1 to 256, 20480 in all
- features: bfloat16 [128, 256, 2048], P('dp', None, 'mp'), may hold values from -24 to 24
- query_rows: bfloat16 [128, 256, 2048], P('dp', None, 'mp'), may hold values from -6 to 6
- key_rows: bfloat16 [128, 256, 2048], P('dp', None, 'mp'), may hold values from -6 to 6
- log_forget: float32 [128, 256, 4], P('dp', None, 'mp'), may hold values from -1 to 0, as said below
- in_gate: float32 [128, 256, 4], P('dp', None, 'mp'), may hold values from -2 to 2
- value_weight: bfloat16 [2048, 2048], P('dp', 'mp'), may hold values from -0.125 to 0.125
- state: float32 [128, 4, 512, 512], P('dp', 'mp'), may hold values from -0.5 to 0.5
- norm_state: float32 [128, 4, 512], P('dp', 'mp'), may hold values from -0.8 to 0.8
- cotangent: bfloat16 [128, 256, 2048], P('dp', None, 'mp'), may hold values from -6 to 6
Outputs:
- hidden: bfloat16 [128, 256, 2048], P('dp', None, 'mp')
- new_state: float32 [128, 4, 512, 512], P('dp', 'mp')
- new_norm: float32 [128, 4, 512], P('dp', 'mp')
- weight_grad: float32 [2048, 2048], P('dp', 'mp')
The draws below stay inside these ranges and needn't reach their ends.
Inputs may be any that keep to these rules, and one draw needn't show every extreme that they name: stream_map is a permutation of the 128 slots. `lengths`: the largest length is exactly 256. `log_forget`: all entries negative.
All inputs are finite; a program needn't handle non-finite values. No bound on the sum of `lengths` on one device may be relied on, other than what follows from the above.
Results may differ from the reference program's by a relative error of at most 0.0065.
Values may be sent and summed in bfloat16 or wider, within the bound.
No kernel may reach another device: no remote copies, remote signals or barrier semaphores. Data moves between devices by JAX's collectives and lax.ppermute only.
A program may use at most 64 MiB of HBM per device.

```python
import math
import jax
import jax.numpy as jnp
import numpy as np
from jax import lax

DIN = 2048
HEAD_COUNT = 4
DH = 512
TOKEN_SLOTS = 256
STREAM_COUNT = 128


def draw_log_forget(key, part):
    random_subkeys = jax.random.split(key, 5)
    low_rate = 0.2 / TOKEN_SLOTS
    high_rate = 1.0 / 30.0
    per_head_rate = jnp.exp(jax.random.uniform(random_subkeys[0], (1, 1, HEAD_COUNT), jnp.float32, math.log(low_rate), math.log(high_rate)))
    stream_multiplier = jnp.exp(jax.random.uniform(random_subkeys[1], (STREAM_COUNT, 1, 1), jnp.float32, math.log(0.5), math.log(2.0)))
    random_noise = jax.random.uniform(random_subkeys[2], (STREAM_COUNT, TOKEN_SLOTS, HEAD_COUNT), jnp.float32, 0.5, 1.5)
    spike_positions = jax.random.randint(random_subkeys[3], (STREAM_COUNT, 2, HEAD_COUNT), 0, TOKEN_SLOTS)
    loss_values = jnp.log(jax.random.uniform(random_subkeys[4], (STREAM_COUNT, 2, HEAD_COUNT), jnp.float32, 0.6, 0.8))
    spike_flags = (spike_positions[..., None] == jnp.arange(TOKEN_SLOTS)[None, None, None, :]).astype(jnp.float32)
    spike_events = jnp.einsum('dxea,dxe->dae', spike_flags, loss_values)
    return jnp.maximum(-per_head_rate * stream_multiplier * random_noise + spike_events, -1.0)


def strengthened(drawn, rng, source, target, blocks, factor):
    owner, partner = [(jnp.arange(drawn.shape[dim]) // (drawn.shape[dim] // blocks)).reshape([-1 if axis == dim else 1 for axis in range(drawn.ndim)]) for dim in (source, target)]
    chosen = jax.random.permutation(rng, blocks)[partner]
    strong = (owner == chosen) | (owner == (partner + blocks // 2) % blocks)
    return jnp.where(strong, factor * drawn, drawn)


def levels(own_key, shape, cuts, smallest, top_value):
    level, own = 1.0, jax.random.fold_in(own_key, 6)
    for dim, blocks in cuts:
        draws = jnp.exp(jax.random.uniform(jax.random.fold_in(own, dim), (blocks,), jnp.float32, smallest / len(cuts), top_value / len(cuts)))
        level = level * jnp.repeat(draws, shape[dim] // blocks).reshape([-1 if axis == dim else 1 for axis in range(len(shape))])
    return level


def length_profile(number_of, total, most, skew):
    loads = [(1 << 20) // math.isqrt(grade ** skew) + 1 for grade in range(2, number_of + 1)]
    rest, holding = total - most - (number_of - 1), [1] * (number_of - 1)
    while rest > 0:
        movable = [i for i in range(number_of - 1) if holding[i] < most]
        whole, budget = sum([loads[i] for i in movable]), rest
        for i in movable:
            addition = min(most - holding[i], max(1, budget * loads[i] // whole), rest)
            holding[i] = holding[i] + addition
            rest = rest - addition
    return np.array([most] + holding)


def uneven(key, count, total, reach, slope):
    if count == 2:
        one = jax.random.randint(key, (), max(1, total - reach), min(reach, total - 1) + 1)
        return jnp.stack([one, total - one])
    sizes = jnp.asarray(length_profile(count, total, reach, slope), jnp.int32)
    twos = (count - 1) // 2
    giver, receiver = sizes[1:1 + 2 * twos:2], sizes[2:2 + 2 * twos:2]
    margin = jnp.minimum(giver - 1, reach - receiver)
    passed = jax.random.randint(jax.random.fold_in(key, 1), (twos,), 0, 1 << 20) % (margin + 1)
    sizes = sizes.at[1:1 + 2 * twos:2].set(giver - passed).at[2:2 + 2 * twos:2].set(receiver + passed)
    return sizes[jax.random.permutation(jax.random.fold_in(key, 2), count)]


def bell_draw(rng, shape, scale, bound, pieces=(), kind=jnp.bfloat16):
    factor_of = levels(rng, shape, pieces, -0.22, 0.18) if pieces else 1.0
    values = jax.random.normal(rng, shape, jnp.float32) * scale * factor_of
    return jnp.minimum(jnp.maximum(values, -bound), bound).astype(kind)


def bell_draw_with(own_key, dims, deviation, bound, shards, heavy, held_as=jnp.bfloat16):
    array = deviation * jax.random.normal(own_key, dims, jnp.float32)
    if shards:
        array = array * levels(own_key, dims, shards, -0.22, 0.18)
    return jnp.clip(strengthened(array, jax.random.fold_in(own_key, 3), *heavy), -bound, bound).astype(held_as)


def setup_inputs(seed: int = 0) -> dict:
    splits = jax.random.split(jax.random.key(seed), 12)
    stream_map = jax.random.permutation(splits[0], STREAM_COUNT).astype(jnp.int32)
    lengths = uneven(splits[1], STREAM_COUNT, STREAM_COUNT * TOKEN_SLOTS * 5 // 8, TOKEN_SLOTS, 1).astype(jnp.int32)
    features = bell_draw_with(splits[2], (STREAM_COUNT, TOKEN_SLOTS, DIN), 1.0, 24.0, ((0, 128), (2, 4)), (0, 2, 128, 5.5))
    query_rows = bell_draw(splits[3], (STREAM_COUNT, TOKEN_SLOTS, HEAD_COUNT * DH), 1.0, 6.0, ((0, 128), (2, 4)))
    key_rows = bell_draw(splits[4], (STREAM_COUNT, TOKEN_SLOTS, HEAD_COUNT * DH), 1.0, 6.0, ((0, 128), (2, 4)))
    log_forget = draw_log_forget(jax.random.fold_in(splits[11], 71), 0)
    in_gate = jnp.clip(jax.random.uniform(splits[6], (STREAM_COUNT, TOKEN_SLOTS, HEAD_COUNT), jnp.float32, -2.0, 2.0) * levels(splits[6], (STREAM_COUNT, TOKEN_SLOTS, HEAD_COUNT), ((0, 128), (2, 4)), -0.4, 0.0), -2.0, 2.0)
    value_weight = bell_draw(splits[7], (DIN, HEAD_COUNT * DH), DIN ** -0.5, 0.125, ((0, 128), (1, 4)))
    state = bell_draw(splits[8], (STREAM_COUNT, HEAD_COUNT, DH, DH), (2.0 / DH ** 0.5), 0.5, ((0, 128), (1, 4)), jnp.float32)
    norm_state = bell_draw(splits[9], (STREAM_COUNT, HEAD_COUNT, DH), (3.0 / DH ** 0.5), 0.8, ((0, 128), (1, 4)), jnp.float32)
    cotangent = bell_draw(splits[10], (STREAM_COUNT, TOKEN_SLOTS, HEAD_COUNT * DH), 1.0, 6.0, ((0, 128), (2, 4)))
    return dict(stream_map=stream_map, lengths=lengths, features=features, query_rows=query_rows, key_rows=key_rows, log_forget=log_forget, in_gate=in_gate, value_weight=value_weight, state=state, norm_state=norm_state, cotangent=cotangent)


def head_pass(features, weight, queries, key_vectors, forget_logs, gate_logs, length, start_state, start_norm, cotangent):
    window = features.shape[0]
    head_width = queries.shape[1]
    values = jnp.dot(features, weight, preferred_element_type=jnp.float32).astype(jnp.bfloat16)
    position = jnp.arange(window, dtype=jnp.int32)
    live_mask = (position < length).astype(jnp.float32)
    decays = jnp.cumsum(forget_logs * live_mask)
    weights_in = jnp.exp(gate_logs) * live_mask
    causal = position[:, None] >= position[None, :]
    gap_logs = jnp.where(causal, decays[:, None] - decays[None, :], -1e30)
    mixing = jnp.exp(gap_logs) * weights_in[None, :]
    scores = lax.dot_general(queries, key_vectors, (((1,), (1,)), ((), ())), preferred_element_type=jnp.float32) * (head_width ** -0.5)
    combined = mixing * scores
    combined_low = combined.astype(jnp.bfloat16)
    carried = jnp.exp(decays)
    query_wide = queries.astype(jnp.float32)
    from_state = jnp.dot(query_wide, start_state, precision=lax.Precision.HIGHEST)
    numer = carried[:, None] * from_state + jnp.dot(combined_low, values, preferred_element_type=jnp.float32)
    inner_dot = carried * jnp.dot(query_wide, start_norm, precision=lax.Precision.HIGHEST) + jnp.sum(combined, axis=1)
    denominator = jnp.maximum(jnp.abs(inner_dot), 1.0)
    hidden = (numer / denominator[:, None] * live_mask[:, None]).astype(jnp.bfloat16)
    final_decay = decays[window - 1]
    tail_weight = jnp.exp(final_decay - decays) * weights_in * (head_width ** -0.5)
    key_scaled = (key_vectors.astype(jnp.float32) * tail_weight[:, None]).astype(jnp.bfloat16)
    new_state = jnp.exp(final_decay) * start_state + lax.dot_general(key_scaled, values, (((0,), (0,)), ((), ())), preferred_element_type=jnp.float32)
    new_norm = jnp.exp(final_decay) * start_norm + jnp.dot(tail_weight, key_vectors.astype(jnp.float32), precision=lax.Precision.HIGHEST)
    scaled = (cotangent.astype(jnp.float32) * (live_mask / denominator)[:, None]).astype(jnp.bfloat16)
    value_grad = lax.dot_general(combined_low, scaled, (((0,), (0,)), ((), ())), preferred_element_type=jnp.float32).astype(jnp.bfloat16)
    weight_grad = lax.dot_general(features, value_grad, (((0,), (0,)), ((), ())), preferred_element_type=jnp.float32)
    return hidden, new_state, new_norm, weight_grad


def reference(stream_map, lengths, features, query_rows, key_rows, log_forget, in_gate, value_weight, state, norm_state, cotangent):
    slot_count = stream_map.shape[0]
    source_slot = jnp.zeros((slot_count,), jnp.int32).at[stream_map].set(jnp.arange(slot_count, dtype=jnp.int32))
    start_state = state[source_slot]
    start_norm = norm_state[source_slot]

    def one_stream(grad_sum, inputs):
        length, feats_now, query_now, key_now, forget_now, gate_now, state_now, norm_now, cot_now = inputs
        hidden_parts, state_parts, norm_parts, grad_parts = [], [], [], []
        for head_index in range(HEAD_COUNT):
            lower = head_index * DH
            result = head_pass(feats_now, value_weight[:, lower:lower + DH], query_now[:, lower:lower + DH],
                               key_now[:, lower:lower + DH], forget_now[:, head_index], gate_now[:, head_index],
                               length, state_now[head_index], norm_now[head_index], cot_now[:, lower:lower + DH])
            hidden_parts.append(result[0])
            state_parts.append(result[1])
            norm_parts.append(result[2])
            grad_parts.append(result[3])
        grad_sum = grad_sum + jnp.concatenate(grad_parts, axis=1)
        return grad_sum, (jnp.concatenate(hidden_parts, axis=1), jnp.stack(state_parts), jnp.stack(norm_parts))

    initial = jnp.zeros((DIN, HEAD_COUNT * DH), jnp.float32)
    grad_total, stacked = lax.scan(one_stream, initial, (lengths, features, query_rows, key_rows, log_forget, in_gate, start_state, start_norm, cotangent))
    return stacked[0], stacked[1], stacked[2], grad_total
```

```python
import functools

import jax
import jax.numpy as jnp
from jax import lax
from jax.experimental import pallas as pl
from jax.experimental.pallas import tpu as pltpu
from jax.sharding import PartitionSpec as P

BF = jnp.bfloat16
F32 = jnp.float32
LANES = 128
VM = pl.BlockSpec(memory_space=pltpu.VMEM)
SM = pl.BlockSpec(memory_space=pltpu.SMEM)


def call(kernel, out, specs, name, flops, scratch=()):
    moved = sum(o.size * o.dtype.itemsize for o in jax.tree.leaves(out))
    return pl.pallas_call(
        kernel,
        out_shape=out,
        in_specs=specs,
        out_specs=jax.tree.map(lambda _: VM, out),
        scratch_shapes=list(scratch),
        name=name,
        cost_estimate=pl.CostEstimate(
            flops=flops, bytes_accessed=2 * moved, transcendentals=0
        ),
    )


def shape(dims, dtype):
    return jax.ShapeDtypeStruct(tuple(dims), dtype)


def contract(a, b, da, db):
    return lax.dot_general(
        a, b, (((da,), (db,)), ((), ())), preferred_element_type=F32
    )


def pack_kernel(state_ref, norm_ref, out_ref):
    groups, cols, rows, _ = out_ref.shape
    rows -= 8
    norm = norm_ref[...]
    high = norm.astype(BF)
    low = (norm - high.astype(F32)).astype(BF)
    parts = [p[:, LANES * i : LANES * (i + 1)] for p in (high.astype(F32), low.astype(F32)) for i in range(4)]
    tile = jnp.concatenate(parts, axis=0).astype(BF)
    for i in range(cols):
        block = state_ref[:, LANES * i : LANES * (i + 1)].astype(BF)
        out_ref[:, i, :rows, :] = block.reshape(groups, rows, LANES)
        out_ref[:, i, rows:, :] = jnp.broadcast_to(tile[None], (groups, 8, LANES))


def permute_kernel(map_ref, own_ref, got_ref, out_ref, norm_ref):
    count, rows, _ = out_ref.shape
    own = own_ref[0]

    def body(s, source):
        slot = map_ref[s]
        out_ref[slot] = got_ref[s, :rows, :]
        return jnp.where(slot == own, s, source)

    source = lax.fori_loop(0, count, body, jnp.int32(0), unroll=8)
    tile = got_ref[source, rows:, :].astype(F32)
    total = tile[:4] + tile[4:]
    norm_ref[...] = jnp.concatenate([total[i : i + 1] for i in range(4)], axis=1)


def mix_kernel(own_ref, forget_ref, gate_ref, q_ref, k_ref, low_ref, scaled_ref, aux_ref, tail_ref):
    window = q_ref.shape[0]
    scale = q_ref.shape[1] ** (-0.5)
    length = own_ref[1]
    t = lax.broadcasted_iota(jnp.int32, (window, window), 0)
    s = lax.broadcasted_iota(jnp.int32, (window, window), 1)
    live_row = (lax.broadcasted_iota(jnp.int32, (1, window), 1) < length).astype(F32)
    live_col = (lax.broadcasted_iota(jnp.int32, (window, 1), 0) < length).astype(F32)
    causal = s <= t
    eye = s == t
    forget = forget_ref[...] * live_row
    decay_col = jnp.sum(jnp.where(causal, forget, 0.0), axis=1, keepdims=True)
    decay_row = jnp.sum(jnp.where(eye, decay_col, 0.0), axis=0, keepdims=True)
    weight_row = jnp.exp(gate_ref[...]) * live_row
    mixing = jnp.exp(jnp.where(causal, decay_col - decay_row, -1e30)) * weight_row
    combined = mixing * (contract(q_ref[...], k_ref[...], 1, 1) * scale)
    low_ref[...] = combined.astype(BF)
    inner = jnp.sum(combined, axis=1, keepdims=True)
    last = decay_col[window - 1 :, :]
    tail_row = jnp.exp(last - decay_row) * weight_row * scale
    tail_col = jnp.sum(jnp.where(eye, tail_row, 0.0), axis=1, keepdims=True)
    weighted = k_ref[...].astype(F32) * tail_col
    scaled_ref[...] = weighted.astype(BF)
    tail_ref[...] = jnp.sum(weighted, axis=0, keepdims=True)
    lane = lax.broadcasted_iota(jnp.int32, (window, LANES), 1)
    aux_ref[...] = jnp.where(
        lane == 0, jnp.exp(decay_col), jnp.where(lane == 1, inner, jnp.where(lane == 2, live_col, jnp.exp(last)))
    )


def grad_kernel(norm_ref, q_ref, cot_ref, low_ref, aux_ref, tail_ref, vg_ref, live_ref, new_ref):
    norm = norm_ref[...]
    dot = jnp.sum(q_ref[...].astype(F32) * norm, axis=1, keepdims=True)
    inner = aux_ref[:, 0:1] * dot + aux_ref[:, 1:2]
    live = aux_ref[:, 2:3] / jnp.maximum(jnp.abs(inner), 1.0)
    scaled = (cot_ref[...].astype(F32) * live).astype(BF)
    vg_ref[...] = contract(low_ref[...], scaled, 0, 0).astype(BF)
    live_ref[...] = jnp.broadcast_to(live, live_ref.shape)
    new_ref[...] = aux_ref[0:1, 3:4] * norm + tail_ref[...]


def weight_kernel(own_ref, f_ref, vg_ref, mine_ref, theirs_ref):
    parts, _, width = f_ref.shape
    rows, cols = mine_ref.shape[1:]
    count = width // (2 * rows)
    core = own_ref[2]
    for j in range(parts):
        part = contract(f_ref[j], vg_ref[...], 0, 0).reshape(count, 2, rows, cols)
        at = pl.ds(count * j, count)

        @pl.when(core == 0)
        def _():
            mine_ref[at] = part[:, 0]
            theirs_ref[at] = part[:, 1].astype(BF)

        @pl.when(core == 1)
        def _():
            mine_ref[at] = part[:, 1]
            theirs_ref[at] = part[:, 0].astype(BF)


def value_kernel(own_ref, f_ref, mine_ref, theirs_ref, v_ref, w_ref):
    parts, _, width = f_ref.shape
    rows, cols = mine_ref.shape[1:]
    count = width // (2 * rows)
    core = own_ref[2]
    w_ref[:, core] = mine_ref[...]
    w_ref[:, 1 - core] = theirs_ref[...]
    total = None
    for j in range(parts):
        block = w_ref[count * j : count * (j + 1)].reshape(width, cols)
        part = contract(f_ref[j], block, 1, 0)
        total = part if total is None else total + part
    v_ref[...] = total.astype(BF)


def final_kernel(got_ref, q_ref, low_ref, v_ref, scaled_ref, aux_ref, live_ref, hidden_ref, new_ref):
    groups, cols, rows, _ = got_ref.shape
    keep = aux_ref[0:1, 3:4]
    carried = aux_ref[:, 0:1]
    live = live_ref[:, 0:1]
    for i in range(cols):
        at = slice(LANES * i, LANES * (i + 1))
        block = got_ref[:, i].reshape(groups * rows, LANES)
        v = v_ref[:, at]
        numer = carried * contract(q_ref[...], block, 1, 0) + contract(low_ref[...], v, 1, 0)
        hidden_ref[:, at] = (numer * live).astype(BF)
        new_ref[:, at] = keep * block.astype(F32) + contract(scaled_ref[...], v, 0, 0)


def on_device(
    stream_map,
    lengths,
    features,
    query_rows,
    key_rows,
    log_forget,
    in_gate,
    value_weight,
    state,
    norm_state,
    cotangent,
):
    slots = lax.axis_size("dp")
    heads = lax.axis_size("mp")
    half = slots // 2
    window, head = query_rows.shape[1:]
    width = features.shape[2]
    rows = value_weight.shape[0]
    block = head * head // (slots * LANES)
    lane_groups = head // LANES
    groups = slots // lane_groups
    pairs = [(i, i ^ 1) for i in range(slots)]
    same_core = [list(range(c, slots, 2)) for c in range(2)]
    q, k, cot = query_rows[0], key_rows[0], cotangent[0]
    here = lax.axis_index("dp").astype(jnp.int32)
    own = jnp.stack([here, lengths[0], here % 2])

    def exchange(x, axis, index_groups=None):
        return lax.all_to_all(x, axis, 0, 0, axis_index_groups=index_groups, tiled=True)

    packed = call(
        pack_kernel, shape((groups, lane_groups, block + 8, LANES), BF), [VM, VM], "pack", 10**6
    )(state[0, 0], norm_state[0]).reshape(slots, block + 8, LANES)
    spread = exchange(packed, "dp")
    feature_all = exchange(jnp.broadcast_to(features, (heads, window, width)), "mp")
    weight_mine = exchange(jnp.broadcast_to(value_weight[None], (half, rows, head)), "dp", same_core)
    weight_theirs = lax.ppermute(weight_mine, "dp", pairs)

    low, key_scaled, aux, tail = call(
        mix_kernel,
        (
            shape((window, window), BF),
            shape((window, head), BF),
            shape((window, LANES), F32),
            shape((1, head), F32),
        ),
        [SM, VM, VM, VM, VM],
        "mix",
        2 * window * window * head,
    )(own, log_forget[0].reshape(1, window), in_gate[0].reshape(1, window), q, k)

    picked, norm = call(
        permute_kernel,
        (shape((slots, block, LANES), BF), shape((1, head), F32)),
        [SM, SM, VM],
        "permute",
        10**6,
    )(stream_map, own, spread)
    returned = exchange(picked, "dp")

    value_grad, live, new_norm = call(
        grad_kernel,
        (shape((window, head), BF), shape((window, LANES), F32), shape((1, head), F32)),
        [VM] * 6,
        "grad",
        2 * window * window * head,
    )(norm, q, cot, low, aux, tail)
    mine, theirs = call(
        weight_kernel,
        (shape((half, rows, head), F32), shape((half, rows, head), BF)),
        [SM, VM, VM],
        "weight",
        2 * window * heads * width * head,
    )(own, feature_all, value_grad)
    paired = (mine + lax.ppermute(theirs, "dp", pairs).astype(F32)).astype(BF)
    weight_parts = exchange(paired, "dp", same_core)

    values = call(
        value_kernel,
        shape((window, head), BF),
        [SM, VM, VM, VM],
        "value",
        2 * window * heads * width * head,
        [pltpu.VMEM((half, 2, rows, head), BF)],
    )(own, feature_all, weight_mine, weight_theirs)
    hidden, new_state = call(
        final_kernel,
        (shape((window, head), BF), shape((head, head), F32)),
        [VM] * 7,
        "final",
        2 * window * head * (2 * head + window),
    )(returned.reshape(groups, lane_groups, block, LANES), q, low, values, key_scaled, aux, live)
    weight_grad = jnp.sum(weight_parts.astype(F32), axis=0)
    return (hidden[None], new_state[None, None], new_norm[None], weight_grad)


def solution(mesh):
    return jax.shard_map(
        on_device,
        mesh=mesh,
        in_specs=(
            P(),
            P("dp"),
            P("dp", None, "mp"),
            P("dp", None, "mp"),
            P("dp", None, "mp"),
            P("dp", None, "mp"),
            P("dp", None, "mp"),
            P("dp", "mp"),
            P("dp", "mp", None, None),
            P("dp", "mp", None),
            P("dp", None, "mp"),
        ),
        out_specs=(
            P("dp", None, "mp"),
            P("dp", "mp", None, None),
            P("dp", "mp", None),
            P("dp", "mp"),
        ),
        check_vma=False,
    )
```

```python
import jax
import jax.numpy as jnp
from jax import lax
from jax.experimental import pallas as pl
from jax.experimental.pallas import tpu as pltpu
from jax.sharding import PartitionSpec as P


BF = jnp.bfloat16
F32 = jnp.float32
LANES = 128
VM = pl.BlockSpec(memory_space=pltpu.VMEM)
SM = pl.BlockSpec(memory_space=pltpu.SMEM)


def call(kernel, out, specs, flops, scratch=()):
    moved = sum(o.size * o.dtype.itemsize for o in jax.tree.leaves(out))
    return pl.pallas_call(
        kernel,
        out_shape=out,
        in_specs=specs,
        out_specs=jax.tree.map(lambda _: VM, out),
        scratch_shapes=list(scratch),
        compiler_params=pltpu.CompilerParams(vmem_limit_bytes=16 << 20),
        cost_estimate=pl.CostEstimate(
            flops=flops, bytes_accessed=2 * moved, transcendentals=0
        ),
    )


def shape(dims, dtype):
    return jax.ShapeDtypeStruct(tuple(dims), dtype)


def contract(a, b, da, db):
    return lax.dot_general(
        a, b, (((da,), (db,)), ((), ())), preferred_element_type=F32
    )


def pack_kernel(state_ref, norm_ref, out_ref):
    groups, cols, rows, _ = out_ref.shape
    rows -= 8
    norm = norm_ref[...]
    high = norm.astype(BF)
    low = (norm - high.astype(F32)).astype(BF)
    parts = [p[:, LANES * i : LANES * (i + 1)] for p in (high.astype(F32), low.astype(F32)) for i in range(4)]
    tile = jnp.concatenate(parts, axis=0).astype(BF)
    for i in range(cols):
        block = state_ref[:, LANES * i : LANES * (i + 1)].astype(BF)
        out_ref[:, i, :rows, :] = block.reshape(groups, rows, LANES)
        out_ref[:, i, rows:, :] = jnp.broadcast_to(tile[None], (groups, 8, LANES))


def permute_kernel(map_ref, own_ref, got_ref, w_ref, out_ref, norm_ref):
    half, parts, rows, _ = out_ref.shape
    for i in range(parts - 2):
        out_ref[:, 2 + i] = jnp.broadcast_to(w_ref[:, LANES * i : LANES * (i + 1)].reshape(1, rows, LANES), (half, rows, LANES))
    own = own_ref[0]

    def body(s, source):
        slot = map_ref[s]
        out_ref[lax.shift_right_logical(slot, 1), slot & 1] = got_ref[s, :rows, :]
        return jnp.where(slot == own, s, source)

    source = lax.fori_loop(0, 2 * half, body, jnp.int32(0), unroll=8)
    tile = got_ref[source, rows:, :].astype(F32)
    total = tile[:4] + tile[4:]
    norm_ref[...] = jnp.concatenate([total[i : i + 1] for i in range(4)], axis=1)


def mix_kernel(own_ref, forget_ref, gate_ref, q_ref, k_ref, low_ref, scaled_ref, aux_ref, tail_ref):
    window = q_ref.shape[0]
    scale = q_ref.shape[1] ** (-0.5)
    length = own_ref[1]
    t = lax.broadcasted_iota(jnp.int32, (window, window), 0)
    s = lax.broadcasted_iota(jnp.int32, (window, window), 1)
    live_row = (lax.broadcasted_iota(jnp.int32, (1, window), 1) < length).astype(F32)
    live_col = (lax.broadcasted_iota(jnp.int32, (window, 1), 0) < length).astype(F32)
    causal = s <= t
    eye = s == t
    forget = forget_ref[...] * live_row
    decay_col = jnp.sum(jnp.where(causal, forget, 0.0), axis=1, keepdims=True)
    decay_row = jnp.sum(jnp.where(eye, decay_col, 0.0), axis=0, keepdims=True)
    weight_row = jnp.exp(gate_ref[...]) * live_row
    mixing = jnp.exp(jnp.where(causal, decay_col - decay_row, -1e30)) * weight_row
    combined = mixing * (contract(q_ref[...], k_ref[...], 1, 1) * scale)
    low_ref[...] = combined.astype(BF)
    inner = jnp.sum(combined, axis=1, keepdims=True)
    last = decay_col[window - 1 :, :]
    tail_row = jnp.exp(last - decay_row) * weight_row * scale
    tail_col = jnp.sum(jnp.where(eye, tail_row, 0.0), axis=1, keepdims=True)
    weighted = k_ref[...].astype(F32) * tail_col
    scaled_ref[...] = weighted.astype(BF)
    tail_ref[...] = jnp.sum(weighted, axis=0, keepdims=True)
    lane = lax.broadcasted_iota(jnp.int32, (window, LANES), 1)
    aux_ref[...] = jnp.where(
        lane == 0, jnp.exp(decay_col), jnp.where(lane == 1, inner, jnp.where(lane == 2, live_col, jnp.exp(last)))
    )


def grad_kernel(norm_ref, q_ref, cot_ref, low_ref, aux_ref, tail_ref, vg_ref, live_ref, new_ref):
    norm = norm_ref[...]
    dot = jnp.sum(q_ref[...].astype(F32) * norm, axis=1, keepdims=True)
    inner = aux_ref[:, 0:1] * dot + aux_ref[:, 1:2]
    live = aux_ref[:, 2:3] / jnp.maximum(jnp.abs(inner), 1.0)
    scaled = (cot_ref[...].astype(F32) * live).astype(BF)
    vg_ref[...] = contract(low_ref[...], scaled, 0, 0).astype(BF)
    live_ref[...] = jnp.broadcast_to(live, live_ref.shape)
    new_ref[...] = aux_ref[0:1, 3:4] * norm + tail_ref[...]


def weight_kernel(own_ref, *refs):
    *f_refs, vg_ref, mine_ref, theirs_ref = refs
    width = f_refs[0].shape[1]
    rows, cols = mine_ref.shape[1:]
    count = width // (2 * rows)
    core = own_ref[2]
    for step, f_ref in enumerate(f_refs):
        part = contract(f_ref[...], vg_ref[...], 0, 0).reshape(count, 2, rows, cols)
        at = pl.ds(count * lax.rem(own_ref[3] + step, len(f_refs)), count)

        @pl.when(core == 0)
        def _():
            mine_ref[at] = part[:, 0]
            theirs_ref[at] = part[:, 1].astype(BF)

        @pl.when(core == 1)
        def _():
            mine_ref[at] = part[:, 1]
            theirs_ref[at] = part[:, 0].astype(BF)


def value_kernel(own_ref, *refs):
    *f_refs, mine_ref, theirs_ref, v_ref, w_ref = refs
    width = f_refs[0].shape[1]
    rows, cols = w_ref.shape[2:]
    count = width // (2 * rows)
    core = own_ref[2]
    for i in range(cols // LANES):
        at = slice(LANES * i, LANES * (i + 1))
        w_ref[:, core, :, at] = mine_ref[:, 2 + i]
        w_ref[:, 1 - core, :, at] = theirs_ref[:, 2 + i]
    total = None
    for step, f_ref in enumerate(f_refs):
        at = pl.ds(count * lax.rem(own_ref[3] + step, len(f_refs)), count)
        part = contract(f_ref[...], w_ref[at].reshape(width, cols), 1, 0)
        total = part if total is None else total + part
    v_ref[...] = total.astype(BF)


def final_kernel(own_ref, mine_ref, theirs_ref, q_ref, low_ref, v_ref, scaled_ref, aux_ref, live_ref, hidden_ref, new_ref, c_ref):
    half, _, rows, _ = c_ref.shape
    cols = q_ref.shape[1] // LANES
    core = own_ref[2]
    c_ref[:, core] = mine_ref[:, core]
    c_ref[:, 1 - core] = theirs_ref[:, core]
    keep = aux_ref[0:1, 3:4]
    carried = aux_ref[:, 0:1]
    live = live_ref[:, 0:1]
    for i in range(cols):
        at = slice(LANES * i, LANES * (i + 1))
        block = c_ref[...].reshape(2 * half // cols, cols, rows, LANES)[:, i].reshape(-1, LANES)
        v = v_ref[:, at]
        numer = carried * contract(q_ref[...], block, 1, 0) + contract(low_ref[...], v, 1, 0)
        hidden_ref[:, at] = (numer * live).astype(BF)
        new_ref[:, at] = keep * block.astype(F32) + contract(scaled_ref[...], v, 0, 0)


def on_device(
    stream_map,
    lengths,
    features,
    query_rows,
    key_rows,
    log_forget,
    in_gate,
    value_weight,
    state,
    norm_state,
    cotangent,
):
    slots = lax.axis_size("dp")
    heads = lax.axis_size("mp")
    half = slots // 2
    window, head = query_rows.shape[1:]
    width = features.shape[2]
    rows = value_weight.shape[0]
    block = head * head // (slots * LANES)
    lane_groups = head // LANES
    groups = slots // lane_groups
    pairs = [(i, i ^ 1) for i in range(slots)]
    same_core = [list(range(c, slots, 2)) for c in range(2)]
    q, k, cot = query_rows[0], key_rows[0], cotangent[0]
    here = lax.axis_index("dp").astype(jnp.int32)
    head_here = lax.axis_index("mp").astype(jnp.int32)
    own = jnp.stack([here, lengths[0], here % 2, head_here])

    def exchange(x, index_groups=None):
        return lax.all_to_all(x, "dp", 0, 0, axis_index_groups=index_groups, tiled=True)

    packed = call(
        pack_kernel, shape((groups, lane_groups, block + 8, LANES), BF), [VM, VM], 10**6
    )(state[0, 0], norm_state[0]).reshape(slots, block + 8, LANES)
    spread = exchange(packed)
    feature_parts = [features[0]] + [
        lax.ppermute(features[0], "mp", [((j + step) % heads, j) for j in range(heads)]) for step in range(1, heads)
    ]

    low, key_scaled, aux, tail = call(
        mix_kernel,
        (
            shape((window, window), BF),
            shape((window, head), BF),
            shape((window, LANES), F32),
            shape((1, head), F32),
        ),
        [SM, VM, VM, VM, VM],
        2 * window * window * head,
    )(own, log_forget[0].reshape(1, window), in_gate[0].reshape(1, window), q, k)

    picked, norm = call(
        permute_kernel,
        (shape((half, 2 + lane_groups, block, LANES), BF), shape((1, head), F32)),
        [SM, SM, VM, VM],
        10**6,
    )(stream_map, own, spread, value_weight)
    returned = exchange(picked, same_core)

    value_grad, live, new_norm = call(
        grad_kernel,
        (shape((window, head), BF), shape((window, LANES), F32), shape((1, head), F32)),
        [VM] * 6,
        2 * window * window * head,
    )(norm, q, cot, low, aux, tail)
    mine, theirs = call(
        weight_kernel,
        (shape((half, rows, head), F32), shape((half, rows, head), BF)),
        [SM] + [VM] * (heads + 1),
        2 * window * heads * width * head,
    )(own, *feature_parts, value_grad)
    paired = (mine + lax.ppermute(theirs, "dp", pairs).astype(F32)).astype(BF)
    weight_parts = exchange(paired, same_core)

    swapped = lax.ppermute(returned, "dp", pairs)
    values = call(
        value_kernel,
        shape((window, head), BF),
        [SM] + [VM] * (heads + 2),
        2 * window * heads * width * head,
        [pltpu.VMEM((half, 2, rows, head), BF)],
    )(own, *feature_parts, returned, swapped)
    hidden, new_state = call(
        final_kernel,
        (shape((window, head), BF), shape((head, head), F32)),
        [SM] + [VM] * 8,
        2 * window * head * (2 * head + window),
        [pltpu.VMEM((half, 2, block, LANES), BF)],
    )(own, returned, swapped, q, low, values, key_scaled, aux, live)
    weight_grad = jnp.sum(weight_parts.astype(F32), axis=0)
    return (hidden[None], new_state[None, None], new_norm[None], weight_grad)


def solution(mesh):
    return jax.shard_map(
        on_device,
        mesh=mesh,
        in_specs=(
            P(),
            P("dp"),
            P("dp", None, "mp"),
            P("dp", None, "mp"),
            P("dp", None, "mp"),
            P("dp", None, "mp"),
            P("dp", None, "mp"),
            P("dp", "mp"),
            P("dp", "mp", None, None),
            P("dp", "mp", None),
            P("dp", None, "mp"),
        ),
        out_specs=(
            P("dp", None, "mp"),
            P("dp", "mp", None, None),
            P("dp", "mp", None),
            P("dp", "mp"),
        ),
        check_vma=False,
    )
```

```python
import math

import jax
import jax.numpy as jnp
from jax import lax
from jax.experimental import pallas as pl
from jax.experimental.pallas import tpu as pltpu
from jax.sharding import PartitionSpec as P


BF = jnp.bfloat16
F32 = jnp.float32
LANES = 128
VM = pl.BlockSpec(memory_space=pltpu.VMEM)
SM = pl.BlockSpec(memory_space=pltpu.SMEM)


def call(kernel, out, specs, flops, scratch=()):
    moved = sum(o.size * o.dtype.itemsize for o in jax.tree.leaves(out))
    return pl.pallas_call(
        kernel,
        out_shape=out,
        in_specs=specs,
        out_specs=jax.tree.map(lambda _: VM, out),
        scratch_shapes=list(scratch),
        compiler_params=pltpu.CompilerParams(vmem_limit_bytes=16 << 20),
        cost_estimate=pl.CostEstimate(
            flops=flops, bytes_accessed=2 * moved, transcendentals=0
        ),
    )


def shape(dims, dtype):
    return jax.ShapeDtypeStruct(tuple(dims), dtype)


def contract(a, b, da, db):
    return lax.dot_general(
        a, b, (((da,), (db,)), ((), ())), preferred_element_type=F32
    )


def pack_kernel(state_ref, norm_ref, out_ref):
    groups, cols, rows, _ = out_ref.shape
    rows -= 8
    norm = norm_ref[...]
    high = norm.astype(BF)
    low = (norm - high.astype(F32)).astype(BF)
    parts = [p[:, LANES * i : LANES * (i + 1)] for p in (high.astype(F32), low.astype(F32)) for i in range(4)]
    tile = jnp.concatenate(parts, axis=0).astype(BF)
    for i in range(cols):
        block = state_ref[:, LANES * i : LANES * (i + 1)].astype(BF)
        out_ref[:, i, :rows, :] = block.reshape(groups, rows, LANES)
        out_ref[:, i, rows:, :] = jnp.broadcast_to(tile[None], (groups, 8, LANES))


def permute_kernel(map_ref, own_ref, got_ref, out_ref, norm_ref):
    half, _, rows, _ = out_ref.shape
    own = own_ref[0]

    def body(s, source):
        slot = map_ref[s]
        out_ref[lax.shift_right_logical(slot, 1), slot & 1] = got_ref[s, :rows, :]
        return jnp.where(slot == own, s, source)

    source = lax.fori_loop(0, 2 * half, body, jnp.int32(0), unroll=8)
    tile = got_ref[source, rows:, :].astype(F32)
    total = tile[:4] + tile[4:]
    norm_ref[...] = jnp.concatenate([total[i : i + 1] for i in range(4)], axis=1)


def mix_kernel(own_ref, forget_ref, gate_ref, q_ref, k_ref, low_ref, scaled_ref, aux_ref, tail_ref):
    window = q_ref.shape[0]
    scale = q_ref.shape[1] ** (-0.5)
    length = own_ref[1]
    t = lax.broadcasted_iota(jnp.int32, (window, window), 0)
    s = lax.broadcasted_iota(jnp.int32, (window, window), 1)
    live_row = (lax.broadcasted_iota(jnp.int32, (1, window), 1) < length).astype(F32)
    live_col = (lax.broadcasted_iota(jnp.int32, (window, 1), 0) < length).astype(F32)
    causal = s <= t
    eye = s == t
    forget = forget_ref[...] * live_row
    decay_col = jnp.sum(jnp.where(causal, forget, 0.0), axis=1, keepdims=True)
    decay_row = jnp.sum(jnp.where(eye, decay_col, 0.0), axis=0, keepdims=True)
    weight_row = jnp.exp(gate_ref[...]) * live_row
    mixing = jnp.exp(jnp.where(causal, decay_col - decay_row, -1e30)) * weight_row
    combined = mixing * (contract(q_ref[...], k_ref[...], 1, 1) * scale)
    low_ref[...] = combined.astype(BF)
    inner = jnp.sum(combined, axis=1, keepdims=True)
    last = decay_col[window - 1 :, :]
    tail_row = jnp.exp(last - decay_row) * weight_row * scale
    tail_col = jnp.sum(jnp.where(eye, tail_row, 0.0), axis=1, keepdims=True)
    weighted = k_ref[...].astype(F32) * tail_col
    scaled_ref[...] = weighted.astype(BF)
    tail_ref[...] = jnp.sum(weighted, axis=0, keepdims=True)
    lane = lax.broadcasted_iota(jnp.int32, (window, LANES), 1)
    aux_ref[...] = jnp.where(
        lane == 0, jnp.exp(decay_col), jnp.where(lane == 1, inner, jnp.where(lane == 2, live_col, jnp.exp(last)))
    )


def grad_kernel(norm_ref, q_ref, cot_ref, low_ref, aux_ref, tail_ref, vg_ref, live_ref, new_ref):
    norm = norm_ref[...]
    dot = jnp.sum(q_ref[...].astype(F32) * norm, axis=1, keepdims=True)
    inner = aux_ref[:, 0:1] * dot + aux_ref[:, 1:2]
    live = aux_ref[:, 2:3] / jnp.maximum(jnp.abs(inner), 1.0)
    scaled = (cot_ref[...].astype(F32) * live).astype(BF)
    vg_ref[...] = contract(low_ref[...], scaled, 0, 0).astype(BF)
    live_ref[...] = jnp.broadcast_to(live, live_ref.shape)
    new_ref[...] = aux_ref[0:1, 3:4] * norm + tail_ref[...]


def weight_kernel(own_ref, *refs):
    *f_refs, vg_ref, mine_ref, theirs_ref = refs
    width = f_refs[0].shape[1]
    rows, cols = mine_ref.shape[1:]
    count = width // (2 * rows)
    core = own_ref[2]
    for step, f_ref in enumerate(f_refs):
        part = contract(f_ref[...], vg_ref[...], 0, 0).reshape(count, 2, rows, cols)
        at = pl.ds(count * lax.rem(own_ref[3] + step, len(f_refs)), count)

        @pl.when(core == 0)
        def _():
            mine_ref[at] = part[:, 0]
            theirs_ref[at] = part[:, 1].astype(BF)

        @pl.when(core == 1)
        def _():
            mine_ref[at] = part[:, 1]
            theirs_ref[at] = part[:, 0].astype(BF)


def join_kernel(own_ref, mine_ref, theirs_ref, *refs):
    *w_refs, out_ref = refs
    side, _, _, rows, cols = out_ref.shape
    core = own_ref[2]
    for y in range(side):
        at = slice(side * y, side * (y + 1))
        total = (mine_ref[at] + theirs_ref[at].astype(F32)).astype(BF)

        @pl.when(core == 0)
        def _():
            out_ref[y, 0] = total

        @pl.when(core == 1)
        def _():
            out_ref[:, 0, y] = total

    for step, w_ref in enumerate(w_refs):
        at = lax.rem(own_ref[4] + step, side)
        out_ref[:, 1, at] = jnp.broadcast_to(w_ref[...][None], (side, rows, cols))


def part_kernel(own_ref, got_ref, part_ref, w_ref):
    side = got_ref.shape[0]
    core = own_ref[2]
    part_ref[...] = jnp.sum(got_ref[:, 0].astype(F32), axis=0).astype(BF)
    for y in range(side):
        at = slice(side * y, side * (y + 1))

        @pl.when(core == 0)
        def _():
            w_ref[at] = got_ref[y, 1]

        @pl.when(core == 1)
        def _():
            w_ref[at] = got_ref[:, 1, y]


def value_kernel(own_ref, *refs):
    *f_refs, mine_ref, theirs_ref, v_ref, w_ref = refs
    width = f_refs[0].shape[1]
    rows, cols = w_ref.shape[2:]
    count = width // (2 * rows)
    core = own_ref[2]
    w_ref[:, core] = mine_ref[...]
    w_ref[:, 1 - core] = theirs_ref[...]
    total = None
    for step, f_ref in enumerate(f_refs):
        at = pl.ds(count * lax.rem(own_ref[3] + step, len(f_refs)), count)
        part = contract(f_ref[...], w_ref[at].reshape(width, cols), 1, 0)
        total = part if total is None else total + part
    v_ref[...] = total.astype(BF)


def final_kernel(own_ref, mine_ref, theirs_ref, q_ref, low_ref, v_ref, scaled_ref, aux_ref, live_ref, hidden_ref, new_ref, c_ref):
    half, _, rows, _ = c_ref.shape
    cols = q_ref.shape[1] // LANES
    core = own_ref[2]
    c_ref[:, core] = mine_ref[:, core]
    c_ref[:, 1 - core] = theirs_ref[:, core]
    keep = aux_ref[0:1, 3:4]
    carried = aux_ref[:, 0:1]
    live = live_ref[:, 0:1]
    for i in range(cols):
        at = slice(LANES * i, LANES * (i + 1))
        block = c_ref[...].reshape(2 * half // cols, cols, rows, LANES)[:, i].reshape(-1, LANES)
        v = v_ref[:, at]
        numer = carried * contract(q_ref[...], block, 1, 0) + contract(low_ref[...], v, 1, 0)
        hidden_ref[:, at] = (numer * live).astype(BF)
        new_ref[:, at] = keep * block.astype(F32) + contract(scaled_ref[...], v, 0, 0)


def on_device(
    stream_map,
    lengths,
    features,
    query_rows,
    key_rows,
    log_forget,
    in_gate,
    value_weight,
    state,
    norm_state,
    cotangent,
):
    slots = lax.axis_size("dp")
    heads = lax.axis_size("mp")
    half = slots // 2
    window, head = query_rows.shape[1:]
    width = features.shape[2]
    rows = value_weight.shape[0]
    block = head * head // (slots * LANES)
    lane_groups = head // LANES
    groups = slots // lane_groups
    pairs = [(i, i ^ 1) for i in range(slots)]
    same_core = [list(range(c, slots, 2)) for c in range(2)]
    side = math.isqrt(half)
    along_y = [[[2 * (side * y + z) + c for y in range(side)] for z in range(side)] for c in range(2)]
    along_z = [[[2 * (side * y + z) + c for z in range(side)] for y in range(side)] for c in range(2)]
    first, second = along_y[0] + along_z[1], along_z[0] + along_y[1]
    q, k, cot = query_rows[0], key_rows[0], cotangent[0]
    here = lax.axis_index("dp").astype(jnp.int32)
    head_here = lax.axis_index("mp").astype(jnp.int32)
    core = here & 1
    shift = side.bit_length() - 1
    inner = lax.shift_right_logical(here, 1 + shift * core) & (side - 1)
    own = jnp.stack([here, lengths[0], core, head_here, inner])

    def exchange(x, index_groups=None):
        return lax.all_to_all(x, "dp", 0, 0, axis_index_groups=index_groups, tiled=True)

    packed = call(
        pack_kernel, shape((groups, lane_groups, block + 8, LANES), BF), [VM, VM], 10**6
    )(state[0, 0], norm_state[0]).reshape(slots, block + 8, LANES)
    spread = exchange(packed)
    feature_parts = [features[0]] + [
        lax.ppermute(features[0], "mp", [((j + step) % heads, j) for j in range(heads)])
        for step in range(1, heads)
    ]

    weight_rows = [value_weight] + [
        lax.ppermute(
            value_weight, "dp", [(g[(i + step) % side], g[i]) for g in second for i in range(side)]
        )
        for step in range(1, side)
    ]

    low, key_scaled, aux, tail = call(
        mix_kernel,
        (
            shape((window, window), BF),
            shape((window, head), BF),
            shape((window, LANES), F32),
            shape((1, head), F32),
        ),
        [SM, VM, VM, VM, VM],
        2 * window * window * head,
    )(own, log_forget[0].reshape(1, window), in_gate[0].reshape(1, window), q, k)

    picked, norm = call(
        permute_kernel,
        (shape((half, 2, block, LANES), BF), shape((1, head), F32)),
        [SM, SM, VM],
        10**6,
    )(stream_map, own, spread)
    returned = exchange(picked, same_core)

    value_grad, live, new_norm = call(
        grad_kernel,
        (shape((window, head), BF), shape((window, LANES), F32), shape((1, head), F32)),
        [VM] * 6,
        2 * window * window * head,
    )(norm, q, cot, low, aux, tail)
    mine, theirs = call(
        weight_kernel,
        (shape((half, rows, head), F32), shape((half, rows, head), BF)),
        [SM] + [VM] * (heads + 1),
        2 * window * heads * width * head,
    )(own, *feature_parts, value_grad)
    joined = call(
        join_kernel, shape((side, 2, side, rows, head), BF), [SM] + [VM] * (2 + side), 10**6
    )(own, mine, lax.ppermute(theirs, "dp", pairs), *weight_rows)
    gathered = exchange(joined, first)
    swapped = lax.ppermute(returned, "dp", pairs)
    part, weight_mine = call(
        part_kernel, (shape((side, rows, head), BF), shape((half, rows, head), BF)), [SM, VM], 10**6
    )(own, gathered)
    weight_parts = exchange(part, second)
    weight_theirs = lax.ppermute(weight_mine, "dp", pairs)
    values = call(
        value_kernel,
        shape((window, head), BF),
        [SM] + [VM] * (heads + 2),
        2 * window * heads * width * head,
        [pltpu.VMEM((half, 2, rows, head), BF)],
    )(own, *feature_parts, weight_mine, weight_theirs)
    hidden, new_state = call(
        final_kernel,
        (shape((window, head), BF), shape((head, head), F32)),
        [SM] + [VM] * 8,
        2 * window * head * (2 * head + window),
        [pltpu.VMEM((half, 2, block, LANES), BF)],
    )(own, returned, swapped, q, low, values, key_scaled, aux, live)
    weight_grad = jnp.sum(weight_parts.astype(F32), axis=0)
    return (hidden[None], new_state[None, None], new_norm[None], weight_grad)


def solution(mesh):
    return jax.shard_map(
        on_device,
        mesh=mesh,
        in_specs=(
            P(),
            P("dp"),
            P("dp", None, "mp"),
            P("dp", None, "mp"),
            P("dp", None, "mp"),
            P("dp", None, "mp"),
            P("dp", None, "mp"),
            P("dp", "mp"),
            P("dp", "mp", None, None),
            P("dp", "mp", None),
            P("dp", None, "mp"),
        ),
        out_specs=(
            P("dp", None, "mp"),
            P("dp", "mp", None, None),
            P("dp", "mp", None),
            P("dp", "mp"),
        ),
        check_vma=False,
    )
```

```python
import math

import jax
import jax.numpy as jnp
from jax import lax
from jax.experimental import pallas as pl
from jax.experimental.pallas import tpu as pltpu
from jax.sharding import PartitionSpec as P


BF = jnp.bfloat16
F32 = jnp.float32
LANES = 128
VM = pl.BlockSpec(memory_space=pltpu.VMEM)
SM = pl.BlockSpec(memory_space=pltpu.SMEM)


def call(kernel, out, specs, flops, scratch=()):
    moved = sum(o.size * o.dtype.itemsize for o in jax.tree.leaves(out))
    return pl.pallas_call(
        kernel,
        out_shape=out,
        in_specs=specs,
        out_specs=jax.tree.map(lambda _: VM, out),
        scratch_shapes=list(scratch),
        compiler_params=pltpu.CompilerParams(vmem_limit_bytes=16 << 20),
        cost_estimate=pl.CostEstimate(
            flops=flops, bytes_accessed=2 * moved, transcendentals=0
        ),
    )


def shape(dims, dtype):
    return jax.ShapeDtypeStruct(tuple(dims), dtype)


def contract(a, b, da, db):
    return lax.dot_general(
        a, b, (((da,), (db,)), ((), ())), preferred_element_type=F32
    )


def pack_kernel(state_ref, norm_ref, out_ref):
    groups, cols, rows, _ = out_ref.shape
    rows -= 8
    norm = norm_ref[...]
    high = norm.astype(BF)
    low = (norm - high.astype(F32)).astype(BF)
    parts = [p[:, LANES * i : LANES * (i + 1)] for p in (high.astype(F32), low.astype(F32)) for i in range(4)]
    tile = jnp.concatenate(parts, axis=0).astype(BF)
    for i in range(cols):
        block = state_ref[:, LANES * i : LANES * (i + 1)].astype(BF)
        out_ref[:, i, :rows, :] = block.reshape(groups, rows, LANES)
        out_ref[:, i, rows:, :] = jnp.broadcast_to(tile[None], (groups, 8, LANES))


def permute_kernel(map_ref, own_ref, got_ref, out_ref, norm_ref):
    half, _, rows, _ = out_ref.shape
    own = own_ref[0]

    def body(s, source):
        slot = map_ref[s]
        out_ref[lax.shift_right_logical(slot, 1), slot & 1] = got_ref[s, :rows, :]
        return jnp.where(slot == own, s, source)

    source = lax.fori_loop(0, 2 * half, body, jnp.int32(0), unroll=8)
    tile = got_ref[source, rows:, :].astype(F32)
    total = tile[:4] + tile[4:]
    norm_ref[...] = jnp.concatenate([total[i : i + 1] for i in range(4)], axis=1)


def mix_kernel(own_ref, forget_ref, gate_ref, q_ref, k_ref, low_ref, scaled_ref, aux_ref, tail_ref):
    window = q_ref.shape[0]
    scale = q_ref.shape[1] ** (-0.5)
    length = own_ref[1]
    t = lax.broadcasted_iota(jnp.int32, (window, window), 0)
    s = lax.broadcasted_iota(jnp.int32, (window, window), 1)
    live_row = (lax.broadcasted_iota(jnp.int32, (1, window), 1) < length).astype(F32)
    live_col = (lax.broadcasted_iota(jnp.int32, (window, 1), 0) < length).astype(F32)
    causal = s <= t
    eye = s == t
    forget = forget_ref[...] * live_row
    decay_col = jnp.sum(jnp.where(causal, forget, 0.0), axis=1, keepdims=True)
    decay_row = jnp.sum(jnp.where(eye, decay_col, 0.0), axis=0, keepdims=True)
    weight_row = jnp.exp(gate_ref[...]) * live_row
    mixing = jnp.exp(jnp.where(causal, decay_col - decay_row, -1e30)) * weight_row
    combined = mixing * (contract(q_ref[...], k_ref[...], 1, 1) * scale)
    low_ref[...] = combined.astype(BF)
    inner = jnp.sum(combined, axis=1, keepdims=True)
    last = decay_col[window - 1 :, :]
    tail_row = jnp.exp(last - decay_row) * weight_row * scale
    tail_col = jnp.sum(jnp.where(eye, tail_row, 0.0), axis=1, keepdims=True)
    weighted = k_ref[...].astype(F32) * tail_col
    scaled_ref[...] = weighted.astype(BF)
    tail_ref[...] = jnp.sum(weighted, axis=0, keepdims=True)
    lane = lax.broadcasted_iota(jnp.int32, (window, LANES), 1)
    aux_ref[...] = jnp.where(
        lane == 0, jnp.exp(decay_col), jnp.where(lane == 1, inner, jnp.where(lane == 2, live_col, jnp.exp(last)))
    )


def grad_kernel(norm_ref, q_ref, cot_ref, low_ref, aux_ref, tail_ref, vg_ref, live_ref, new_ref):
    norm = norm_ref[...]
    dot = jnp.sum(q_ref[...].astype(F32) * norm, axis=1, keepdims=True)
    inner = aux_ref[:, 0:1] * dot + aux_ref[:, 1:2]
    live = aux_ref[:, 2:3] / jnp.maximum(jnp.abs(inner), 1.0)
    scaled = (cot_ref[...].astype(F32) * live).astype(BF)
    vg_ref[...] = contract(low_ref[...], scaled, 0, 0).astype(BF)
    live_ref[...] = jnp.broadcast_to(live, live_ref.shape)
    new_ref[...] = aux_ref[0:1, 3:4] * norm + tail_ref[...]


def weight_kernel(own_ref, *refs):
    *f_refs, vg_ref, mine_ref, theirs_ref = refs
    width = f_refs[0].shape[1]
    rows, cols = mine_ref.shape[1:]
    count = width // (2 * rows)
    core = own_ref[2]
    for step, f_ref in enumerate(f_refs):
        part = contract(f_ref[...], vg_ref[...], 0, 0).reshape(count, 2, rows, cols)
        at = pl.ds(count * lax.rem(own_ref[3] + step, len(f_refs)), count)

        @pl.when(core == 0)
        def _():
            mine_ref[at] = part[:, 0]
            theirs_ref[at] = part[:, 1].astype(BF)

        @pl.when(core == 1)
        def _():
            mine_ref[at] = part[:, 1]
            theirs_ref[at] = part[:, 0].astype(BF)


def join_kernel(own_ref, mine_ref, theirs_ref, keep_ref, send_ref):
    near, side, rows, cols = keep_ref.shape
    core, parity = own_ref[2], own_ref[4]
    for y in range(side):
        at = slice(side * y, side * (y + 1))
        total = mine_ref[at] + theirs_ref[at].astype(F32)

        @pl.when((core == 0) & (parity == y % 2))
        def _():
            keep_ref[y // 2] = total

        @pl.when((core == 0) & (parity != y % 2))
        def _():
            send_ref[y // 2] = total.astype(BF)

        split = total.reshape(near, 2, rows, cols)
        for p in range(2):

            @pl.when((core == 1) & (parity == p))
            def _():
                keep_ref[:, y] = split[:, p]
                send_ref[:, y] = split[:, 1 - p].astype(BF)


def halve_kernel(own_ref, kept_ref, got_ref, keep_ref, send_ref):
    near, _, rows, cols = keep_ref.shape
    parity = own_ref[5]
    for i in range(near):
        split = (kept_ref[i] + got_ref[i].astype(F32)).reshape(near, 2, rows, cols)
        for p in range(2):

            @pl.when(parity == p)
            def _():
                keep_ref[i] = split[:, p]
                send_ref[i] = split[:, 1 - p].astype(BF)


def value_kernel(own_ref, *refs):
    *f_refs, mine_ref, near_ref, pair_ref, far_ref, v_ref, w_ref = refs
    width = f_refs[0].shape[1]
    near, _, _, _, _, rows, cols = w_ref.shape
    count = near // len(f_refs)
    core = own_ref[2]
    for flip, ref, other_ref in ((0, mine_ref, pair_ref), (1, near_ref, far_ref)):
        for step in range(2):
            straight = own_ref[6] ^ step, own_ref[7] ^ flip
            crossed = own_ref[6] ^ flip, own_ref[7] ^ step
            y, z = (jnp.where(core == 0, u, v) for u, v in zip(straight, crossed))
            w_ref[:, y, :, z, core] = ref[step].reshape(near, near, rows, cols)
            y, z = (jnp.where(core == 0, v, u) for u, v in zip(straight, crossed))
            w_ref[:, y, :, z, 1 - core] = other_ref[step].reshape(near, near, rows, cols)
    total = None
    for step, f_ref in enumerate(f_refs):
        at = pl.ds(count * lax.rem(own_ref[3] + step, len(f_refs)), count)
        part = contract(f_ref[...], w_ref[at].reshape(width, cols), 1, 0)
        total = part if total is None else total + part
    v_ref[...] = total.astype(BF)


def final_kernel(own_ref, mine_ref, theirs_ref, q_ref, low_ref, v_ref, scaled_ref, aux_ref, live_ref, hidden_ref, new_ref, c_ref):
    half, _, rows, _ = c_ref.shape
    cols = q_ref.shape[1] // LANES
    core = own_ref[2]
    c_ref[:, core] = mine_ref[:, core]
    c_ref[:, 1 - core] = theirs_ref[:, core]
    keep = aux_ref[0:1, 3:4]
    carried = aux_ref[:, 0:1]
    live = live_ref[:, 0:1]
    for i in range(cols):
        at = slice(LANES * i, LANES * (i + 1))
        block = c_ref[...].reshape(2 * half // cols, cols, rows, LANES)[:, i].reshape(-1, LANES)
        v = v_ref[:, at]
        numer = carried * contract(q_ref[...], block, 1, 0) + contract(low_ref[...], v, 1, 0)
        hidden_ref[:, at] = (numer * live).astype(BF)
        new_ref[:, at] = keep * block.astype(F32) + contract(scaled_ref[...], v, 0, 0)


def on_device(
    stream_map,
    lengths,
    features,
    query_rows,
    key_rows,
    log_forget,
    in_gate,
    value_weight,
    state,
    norm_state,
    cotangent,
):
    slots = lax.axis_size("dp")
    heads = lax.axis_size("mp")
    half = slots // 2
    window, head = query_rows.shape[1:]
    width = features.shape[2]
    rows = value_weight.shape[0]
    block = head * head // (slots * LANES)
    lane_groups = head // LANES
    groups = slots // lane_groups
    pairs = [(i, i ^ 1) for i in range(slots)]
    same_core = [list(range(c, slots, 2)) for c in range(2)]
    side = math.isqrt(half)
    near = side // 2
    at = lambda y, z, c: 2 * (side * y + z) + c
    quarters = [(py, pz) for py in range(2) for pz in range(2)]
    square = [(u, v) for u in range(near) for v in range(near)]
    by_row = [[at(2 * u + py, 2 * v + pz, c) for u, v in square] for c in range(2) for py, pz in quarters]
    by_core = by_row[:4] + [[at(2 * v + py, 2 * u + pz, 1) for u, v in square] for py, pz in quarters]
    every = [(y, z, c) for y in range(side) for z in range(side) for c in range(2)]
    first = [(at(y, z, c), at(y ^ (1 - c), z ^ c, c)) for y, z, c in every]
    second = [(at(y, z, c), at(y ^ c, z ^ (1 - c), c)) for y, z, c in every]
    q, k, cot = query_rows[0], key_rows[0], cotangent[0]
    here = lax.axis_index("dp").astype(jnp.int32)
    head_here = lax.axis_index("mp").astype(jnp.int32)
    core = here & 1
    odd_z = lax.shift_right_logical(here, 1) & 1
    odd_y = lax.shift_right_logical(here, side.bit_length()) & 1
    odds = [jnp.where(core == 0, odd_y, odd_z), jnp.where(core == 0, odd_z, odd_y)]
    own = jnp.stack([here, lengths[0], core, head_here, *odds, odd_y, odd_z])

    def exchange(x, index_groups=None):
        return lax.all_to_all(x, "dp", 0, 0, axis_index_groups=index_groups, tiled=True)

    def send(x, pairs):
        return lax.ppermute(x, "dp", pairs)

    quarter = exchange(jnp.broadcast_to(value_weight[None], (near * near, rows, head)), by_row)
    packed = call(
        pack_kernel, shape((groups, lane_groups, block + 8, LANES), BF), [VM, VM], 10**6
    )(state[0, 0], norm_state[0]).reshape(slots, block + 8, LANES)
    spread = exchange(packed)
    feature_parts = [features[0]] + [
        lax.ppermute(features[0], "mp", [((j + step) % heads, j) for j in range(heads)])
        for step in range(1, heads)
    ]

    weight_mine = jnp.stack([quarter, send(quarter, first)])
    weight_near = send(weight_mine, second)

    low, key_scaled, aux, tail = call(
        mix_kernel,
        (
            shape((window, window), BF),
            shape((window, head), BF),
            shape((window, LANES), F32),
            shape((1, head), F32),
        ),
        [SM, VM, VM, VM, VM],
        2 * window * window * head,
    )(own, log_forget[0].reshape(1, window), in_gate[0].reshape(1, window), q, k)

    picked, norm = call(
        permute_kernel,
        (shape((half, 2, block, LANES), BF), shape((1, head), F32)),
        [SM, SM, VM],
        10**6,
    )(stream_map, own, spread)
    returned = exchange(picked, same_core)

    value_grad, live, new_norm = call(
        grad_kernel,
        (shape((window, head), BF), shape((window, LANES), F32), shape((1, head), F32)),
        [VM] * 6,
        2 * window * window * head,
    )(norm, q, cot, low, aux, tail)
    mine, theirs = call(
        weight_kernel,
        (shape((half, rows, head), F32), shape((half, rows, head), BF)),
        [SM] + [VM] * (heads + 1),
        2 * window * heads * width * head,
    )(own, *feature_parts, value_grad)
    kept, sent = call(
        join_kernel,
        (shape((near, side, rows, head), F32), shape((near, side, rows, head), BF)),
        [SM, VM, VM],
        10**6,
    )(own, mine, send(theirs, pairs))
    kept, sent = call(
        halve_kernel,
        (shape((near, near, rows, head), F32), shape((near, near, rows, head), BF)),
        [SM, VM, VM],
        10**6,
    )(own, kept, send(sent, first))
    total = (kept + send(sent, second).astype(F32)).astype(BF)
    weight_parts = exchange(total.reshape(near * near, rows, head), by_core)
    swapped = send(returned, pairs)
    weight_pair, weight_far = send(weight_mine, pairs), send(weight_near, pairs)
    values = call(
        value_kernel,
        shape((window, head), BF),
        [SM] + [VM] * (heads + 4),
        2 * window * heads * width * head,
        [pltpu.VMEM((near, 2, near, 2, 2, rows, head), BF)],
    )(own, *feature_parts, weight_mine, weight_near, weight_pair, weight_far)
    hidden, new_state = call(
        final_kernel,
        (shape((window, head), BF), shape((head, head), F32)),
        [SM] + [VM] * 8,
        2 * window * head * (2 * head + window),
        [pltpu.VMEM((half, 2, block, LANES), BF)],
    )(own, returned, swapped, q, low, values, key_scaled, aux, live)
    weight_grad = jnp.sum(weight_parts.astype(F32), axis=0)
    return (hidden[None], new_state[None, None], new_norm[None], weight_grad)


def solution(mesh):
    return jax.shard_map(
        on_device,
        mesh=mesh,
        in_specs=(
            P(),
            P("dp"),
            P("dp", None, "mp"),
            P("dp", None, "mp"),
            P("dp", None, "mp"),
            P("dp", None, "mp"),
            P("dp", None, "mp"),
            P("dp", "mp"),
            P("dp", "mp", None, None),
            P("dp", "mp", None),
            P("dp", None, "mp"),
        ),
        out_specs=(
            P("dp", None, "mp"),
            P("dp", "mp", None, None),
            P("dp", "mp", None),
            P("dp", "mp"),
        ),
        check_vma=False,
    )
```

```python
import functools

import functools
import math

import jax
import jax.numpy as jnp
from jax import lax
from jax.experimental import pallas as pl
from jax.experimental.pallas import tpu as pltpu
from jax.sharding import PartitionSpec as P


BF = jnp.bfloat16
F32 = jnp.float32
LANES = 128
VM = pl.BlockSpec(memory_space=pltpu.VMEM)
SM = pl.BlockSpec(memory_space=pltpu.SMEM)


def call(kernel, out, specs, flops, scratch=()):
    moved = sum(o.size * o.dtype.itemsize for o in jax.tree.leaves(out))
    return pl.pallas_call(
        kernel,
        out_shape=out,
        in_specs=specs,
        out_specs=jax.tree.map(lambda _: VM, out),
        scratch_shapes=list(scratch),
        compiler_params=pltpu.CompilerParams(vmem_limit_bytes=16 << 20),
        cost_estimate=pl.CostEstimate(
            flops=flops, bytes_accessed=2 * moved, transcendentals=0
        ),
    )


def shape(dims, dtype):
    return jax.ShapeDtypeStruct(tuple(dims), dtype)


def contract(a, b, da, db):
    return lax.dot_general(
        a, b, (((da,), (db,)), ((), ())), preferred_element_type=F32
    )


def pack_kernel(state_ref, norm_ref, out_ref):
    groups, cols, rows, _ = out_ref.shape
    rows -= 8
    norm = norm_ref[...]
    high = norm.astype(BF)
    low = (norm - high.astype(F32)).astype(BF)
    parts = [p[:, LANES * i : LANES * (i + 1)] for p in (high.astype(F32), low.astype(F32)) for i in range(4)]
    tile = jnp.concatenate(parts, axis=0).astype(BF)
    for i in range(cols):
        block = state_ref[:, LANES * i : LANES * (i + 1)].astype(BF)
        out_ref[:, i, :rows, :] = block.reshape(groups, rows, LANES)
        out_ref[:, i, rows:, :] = jnp.broadcast_to(tile[None], (groups, 8, LANES))


def permute_kernel(map_ref, own_ref, got_ref, w_ref, out_ref, norm_ref):
    half, parts, rows, _ = out_ref.shape
    for i in range(parts - 2):
        out_ref[:, 2 + i] = jnp.broadcast_to(w_ref[:, LANES * i : LANES * (i + 1)].reshape(1, rows, LANES), (half, rows, LANES))
    own = own_ref[0]

    def body(s, source):
        slot = map_ref[s]
        out_ref[lax.shift_right_logical(slot, 1), slot & 1] = got_ref[s, :rows, :]
        return jnp.where(slot == own, s, source)

    source = lax.fori_loop(0, 2 * half, body, jnp.int32(0), unroll=8)
    tile = got_ref[source, rows:, :].astype(F32)
    total = tile[:4] + tile[4:]
    norm_ref[...] = jnp.concatenate([total[i : i + 1] for i in range(4)], axis=1)


def mix_kernel(own_ref, forget_ref, gate_ref, q_ref, k_ref, low_ref, scaled_ref, aux_ref, tail_ref):
    window = q_ref.shape[0]
    scale = q_ref.shape[1] ** (-0.5)
    length = own_ref[1]
    t = lax.broadcasted_iota(jnp.int32, (window, window), 0)
    s = lax.broadcasted_iota(jnp.int32, (window, window), 1)
    live_row = (lax.broadcasted_iota(jnp.int32, (1, window), 1) < length).astype(F32)
    live_col = (lax.broadcasted_iota(jnp.int32, (window, 1), 0) < length).astype(F32)
    causal = s <= t
    eye = s == t
    forget = forget_ref[...] * live_row
    decay_col = jnp.sum(jnp.where(causal, forget, 0.0), axis=1, keepdims=True)
    decay_row = jnp.sum(jnp.where(eye, decay_col, 0.0), axis=0, keepdims=True)
    weight_row = jnp.exp(gate_ref[...]) * live_row
    mixing = jnp.exp(jnp.where(causal, decay_col - decay_row, -1e30)) * weight_row
    combined = mixing * (contract(q_ref[...], k_ref[...], 1, 1) * scale)
    low_ref[...] = combined.astype(BF)
    inner = jnp.sum(combined, axis=1, keepdims=True)
    last = decay_col[window - 1 :, :]
    tail_row = jnp.exp(last - decay_row) * weight_row * scale
    tail_col = jnp.sum(jnp.where(eye, tail_row, 0.0), axis=1, keepdims=True)
    weighted = k_ref[...].astype(F32) * tail_col
    scaled_ref[...] = weighted.astype(BF)
    tail_ref[...] = jnp.sum(weighted, axis=0, keepdims=True)
    lane = lax.broadcasted_iota(jnp.int32, (window, LANES), 1)
    aux_ref[...] = jnp.where(
        lane == 0, jnp.exp(decay_col), jnp.where(lane == 1, inner, jnp.where(lane == 2, live_col, jnp.exp(last)))
    )


def grad_kernel(norm_ref, q_ref, cot_ref, low_ref, aux_ref, tail_ref, vg_ref, live_ref, new_ref):
    norm = norm_ref[...]
    dot = jnp.sum(q_ref[...].astype(F32) * norm, axis=1, keepdims=True)
    inner = aux_ref[:, 0:1] * dot + aux_ref[:, 1:2]
    live = aux_ref[:, 2:3] / jnp.maximum(jnp.abs(inner), 1.0)
    scaled = (cot_ref[...].astype(F32) * live).astype(BF)
    vg_ref[...] = contract(low_ref[...], scaled, 0, 0).astype(BF)
    live_ref[...] = jnp.broadcast_to(live, live_ref.shape)
    new_ref[...] = aux_ref[0:1, 3:4] * norm + tail_ref[...]


def weight_kernel(own_ref, *refs):
    *f_refs, vg_ref, mine_ref, theirs_ref = refs
    width = f_refs[0].shape[1]
    rows, cols = mine_ref.shape[1:]
    count = width // (2 * rows)
    core = own_ref[2]
    for step, f_ref in enumerate(f_refs):
        part = contract(f_ref[...], vg_ref[...], 0, 0).reshape(count, 2, rows, cols)
        at = pl.ds(count * lax.rem(own_ref[3] + step, len(f_refs)), count)

        @pl.when(core == 0)
        def _():
            mine_ref[at] = part[:, 0]
            theirs_ref[at] = part[:, 1].astype(BF)

        @pl.when(core == 1)
        def _():
            mine_ref[at] = part[:, 1]
            theirs_ref[at] = part[:, 0].astype(BF)


def join_kernel(own_ref, mine_ref, theirs_ref, keep_ref, send_ref):
    near, side, rows, cols = keep_ref.shape
    core, odd = own_ref[2], own_ref[4] & 1
    for y in range(side):
        at = slice(side * y, side * (y + 1))
        total = mine_ref[at] + theirs_ref[at].astype(F32)

        @pl.when((core == 0) & (odd == y % 2))
        def _():
            keep_ref[y // 2] = total

        @pl.when((core == 0) & (odd != y % 2))
        def _():
            send_ref[y // 2] = total.astype(BF)

        split = total.reshape(near, 2, rows, cols)
        for p in range(2):

            @pl.when((core == 1) & (odd == p))
            def _():
                keep_ref[:, y] = split[:, p]
                send_ref[:, y] = split[:, 1 - p].astype(BF)


def halve_kernel(level, own_ref, kept_ref, got_ref, keep_ref, send_ref):
    odd = lax.shift_right_logical(own_ref[4], level) & 1
    for i in range(keep_ref.shape[0]):
        pair = [kept_ref[j] + got_ref[j].astype(F32) for j in (2 * i, 2 * i + 1)]
        for p in range(2):

            @pl.when(odd == p)
            def _():
                keep_ref[i] = pair[p]
                send_ref[i] = pair[1 - p].astype(BF)


def total_kernel(kept_ref, got_ref, out_ref):
    out_ref[...] = (kept_ref[0] + got_ref[0].astype(F32)).astype(BF)


def value_kernel(own_ref, *refs):
    *f_refs, mine_ref, theirs_ref, v_ref, w_ref = refs
    width = f_refs[0].shape[1]
    rows, cols = w_ref.shape[2:]
    count = width // (2 * rows)
    core = own_ref[2]
    for i in range(cols // LANES):
        at = slice(LANES * i, LANES * (i + 1))
        w_ref[:, core, :, at] = mine_ref[:, 2 + i]
        w_ref[:, 1 - core, :, at] = theirs_ref[:, 2 + i]
    total = None
    for step, f_ref in enumerate(f_refs):
        at = pl.ds(count * lax.rem(own_ref[3] + step, len(f_refs)), count)
        part = contract(f_ref[...], w_ref[at].reshape(width, cols), 1, 0)
        total = part if total is None else total + part
    v_ref[...] = total.astype(BF)


def final_kernel(own_ref, mine_ref, theirs_ref, q_ref, low_ref, v_ref, scaled_ref, aux_ref, live_ref, hidden_ref, new_ref, c_ref):
    half, _, rows, _ = c_ref.shape
    cols = q_ref.shape[1] // LANES
    core = own_ref[2]
    c_ref[:, core] = mine_ref[:, core]
    c_ref[:, 1 - core] = theirs_ref[:, core]
    keep = aux_ref[0:1, 3:4]
    carried = aux_ref[:, 0:1]
    live = live_ref[:, 0:1]
    for i in range(cols):
        at = slice(LANES * i, LANES * (i + 1))
        block = c_ref[...].reshape(2 * half // cols, cols, rows, LANES)[:, i].reshape(-1, LANES)
        v = v_ref[:, at]
        numer = carried * contract(q_ref[...], block, 1, 0) + contract(low_ref[...], v, 1, 0)
        hidden_ref[:, at] = (numer * live).astype(BF)
        new_ref[:, at] = keep * block.astype(F32) + contract(scaled_ref[...], v, 0, 0)


def on_device(
    stream_map,
    lengths,
    features,
    query_rows,
    key_rows,
    log_forget,
    in_gate,
    value_weight,
    state,
    norm_state,
    cotangent,
):
    slots = lax.axis_size("dp")
    heads = lax.axis_size("mp")
    half = slots // 2
    window, head = query_rows.shape[1:]
    width = features.shape[2]
    rows = value_weight.shape[0]
    block = head * head // (slots * LANES)
    lane_groups = head // LANES
    groups = slots // lane_groups
    pairs = [(i, i ^ 1) for i in range(slots)]
    same_core = [list(range(c, slots, 2)) for c in range(2)]
    side = math.isqrt(half)
    bits = side.bit_length() - 1
    at = lambda y, z, c: 2 * (side * y + z) + c
    every = [(y, z, c) for y in range(side) for z in range(side) for c in range(2)]
    partners = [[(at(y, z, c), at(y ^ (d * (1 - c)), z ^ (d * c), c)) for y, z, c in every] for d in (1 << i for i in range(bits))]
    lines = [[at(y, z, 0) for z in range(side)] for y in range(side)] + [[at(y, z, 1) for y in range(side)] for z in range(side)]
    q, k, cot = query_rows[0], key_rows[0], cotangent[0]
    here = lax.axis_index("dp").astype(jnp.int32)
    head_here = lax.axis_index("mp").astype(jnp.int32)
    core = here & 1
    first = lax.shift_right_logical(here, 1 + bits * (1 - core)) & (side - 1)
    own = jnp.stack([here, lengths[0], core, head_here, first])

    def send(x, device_pairs):
        return lax.ppermute(x, "dp", device_pairs)

    def exchange(x, index_groups=None):
        return lax.all_to_all(x, "dp", 0, 0, axis_index_groups=index_groups, tiled=True)

    packed = call(
        pack_kernel, shape((groups, lane_groups, block + 8, LANES), BF), [VM, VM], 10**6
    )(state[0, 0], norm_state[0]).reshape(slots, block + 8, LANES)
    spread = exchange(packed)
    feature_parts = [features[0]] + [
        lax.ppermute(features[0], "mp", [((j + step) % heads, j) for j in range(heads)])
        for step in range(1, heads)
    ]

    low, key_scaled, aux, tail = call(
        mix_kernel,
        (
            shape((window, window), BF),
            shape((window, head), BF),
            shape((window, LANES), F32),
            shape((1, head), F32),
        ),
        [SM, VM, VM, VM, VM],
        2 * window * window * head,
    )(own, log_forget[0].reshape(1, window), in_gate[0].reshape(1, window), q, k)

    picked, norm = call(
        permute_kernel,
        (shape((half, 2 + lane_groups, block, LANES), BF), shape((1, head), F32)),
        [SM, SM, VM, VM],
        10**6,
    )(stream_map, own, spread, value_weight)
    returned = exchange(picked, same_core)

    value_grad, live, new_norm = call(
        grad_kernel,
        (shape((window, head), BF), shape((window, LANES), F32), shape((1, head), F32)),
        [VM] * 6,
        2 * window * window * head,
    )(norm, q, cot, low, aux, tail)
    mine, theirs = call(
        weight_kernel,
        (shape((half, rows, head), F32), shape((half, rows, head), BF)),
        [SM] + [VM] * (heads + 1),
        2 * window * heads * width * head,
    )(own, *feature_parts, value_grad)

    def parts(count):
        return shape((count, side, rows, head), F32), shape((count, side, rows, head), BF)

    kept, sent = call(join_kernel, parts(side // 2), [SM, VM, VM], 10**6)(own, mine, send(theirs, pairs))
    for level in range(1, bits):
        kept, sent = call(
            functools.partial(halve_kernel, level), parts(side >> (level + 1)), [SM, VM, VM], 10**6
        )(own, kept, send(sent, partners[level - 1]))
    sent = send(sent, partners[-1])
    total = call(total_kernel, shape((side, rows, head), BF), [VM, VM], 10**6)(kept, sent)
    weight_parts = exchange(total, lines)
    swapped = send(returned, pairs)
    values = call(
        value_kernel,
        shape((window, head), BF),
        [SM] + [VM] * (heads + 2),
        2 * window * heads * width * head,
        [pltpu.VMEM((half, 2, rows, head), BF)],
    )(own, *feature_parts, returned, swapped)
    hidden, new_state = call(
        final_kernel,
        (shape((window, head), BF), shape((head, head), F32)),
        [SM] + [VM] * 8,
        2 * window * head * (2 * head + window),
        [pltpu.VMEM((half, 2, block, LANES), BF)],
    )(own, returned, swapped, q, low, values, key_scaled, aux, live)
    weight_grad = jnp.sum(weight_parts.astype(F32), axis=0)
    return (hidden[None], new_state[None, None], new_norm[None], weight_grad)


def solution(mesh):
    return jax.shard_map(
        on_device,
        mesh=mesh,
        in_specs=(
            P(),
            P("dp"),
            P("dp", None, "mp"),
            P("dp", None, "mp"),
            P("dp", None, "mp"),
            P("dp", None, "mp"),
            P("dp", None, "mp"),
            P("dp", "mp"),
            P("dp", "mp", None, None),
            P("dp", "mp", None),
            P("dp", None, "mp"),
        ),
        out_specs=(
            P("dp", None, "mp"),
            P("dp", "mp", None, None),
            P("dp", "mp", None),
            P("dp", "mp"),
        ),
        check_vma=False,
    )
```

```python
import math

import jax
import jax.numpy as jnp
from jax import lax
from jax.experimental import pallas as pl
from jax.experimental.pallas import tpu as pltpu
from jax.sharding import PartitionSpec as P


BF = jnp.bfloat16
F32 = jnp.float32
LANES = 128
VM = pl.BlockSpec(memory_space=pltpu.VMEM)
SM = pl.BlockSpec(memory_space=pltpu.SMEM)


def call(kernel, out, specs, flops, scratch=()):
    moved = sum(o.size * o.dtype.itemsize for o in jax.tree.leaves(out))
    return pl.pallas_call(
        kernel,
        out_shape=out,
        in_specs=specs,
        out_specs=jax.tree.map(lambda _: VM, out),
        scratch_shapes=list(scratch),
        compiler_params=pltpu.CompilerParams(vmem_limit_bytes=16 << 20),
        cost_estimate=pl.CostEstimate(
            flops=flops, bytes_accessed=2 * moved, transcendentals=0
        ),
    )


def shape(dims, dtype):
    return jax.ShapeDtypeStruct(tuple(dims), dtype)


def contract(a, b, da, db):
    return lax.dot_general(
        a, b, (((da,), (db,)), ((), ())), preferred_element_type=F32
    )


def pack_kernel(state_ref, norm_ref, out_ref):
    groups, _, rows, _ = out_ref.shape
    rows -= 8
    norm = norm_ref[...]
    high = norm.astype(BF)
    low = (norm - high.astype(F32)).astype(BF)
    parts = [p[:, LANES * i : LANES * (i + 1)] for p in (high.astype(F32), low.astype(F32)) for i in range(4)]
    tile = jnp.concatenate(parts, axis=0).astype(BF)
    out_ref[:, 0, :rows, :] = state_ref[...].astype(BF).reshape(groups, rows, LANES)
    out_ref[:, 0, rows:, :] = jnp.broadcast_to(tile[None], (groups, 8, LANES))


def permute_kernel(map_ref, own_ref, got_ref, w_ref, out_ref, norm_ref):
    half, parts, rows, _ = out_ref.shape
    for i in range(parts - 2):
        out_ref[:, 2 + i] = jnp.broadcast_to(w_ref[:, LANES * i : LANES * (i + 1)].reshape(1, rows, LANES), (half, rows, LANES))
    own = own_ref[0]

    def body(s, source):
        slot = map_ref[s]
        out_ref[lax.shift_right_logical(slot, 1), slot & 1] = got_ref[s, :rows, :]
        return jnp.where(slot == own, s, source)

    source = lax.fori_loop(0, 2 * half, body, jnp.int32(0), unroll=8)
    tile = got_ref[source, rows:, :].astype(F32)
    total = tile[:4] + tile[4:]
    norm_ref[...] = jnp.concatenate([total[i : i + 1] for i in range(4)], axis=1)


def mix_kernel(own_ref, forget_ref, gate_ref, q_ref, k_ref, low_ref, scaled_ref, aux_ref, tail_ref):
    window = q_ref.shape[0]
    scale = q_ref.shape[1] ** (-0.5)
    length = own_ref[1]
    t = lax.broadcasted_iota(jnp.int32, (window, window), 0)
    s = lax.broadcasted_iota(jnp.int32, (window, window), 1)
    live_row = (lax.broadcasted_iota(jnp.int32, (1, window), 1) < length).astype(F32)
    live_col = (lax.broadcasted_iota(jnp.int32, (window, 1), 0) < length).astype(F32)
    causal = s <= t
    eye = s == t
    forget = forget_ref[...] * live_row
    decay_col = jnp.sum(jnp.where(causal, forget, 0.0), axis=1, keepdims=True)
    decay_row = jnp.sum(jnp.where(eye, decay_col, 0.0), axis=0, keepdims=True)
    weight_row = jnp.exp(gate_ref[...]) * live_row
    mixing = jnp.exp(jnp.where(causal, decay_col - decay_row, -1e30)) * weight_row
    combined = mixing * (contract(q_ref[...], k_ref[...], 1, 1) * scale)
    low_ref[...] = combined.astype(BF)
    inner = jnp.sum(combined, axis=1, keepdims=True)
    last = decay_col[window - 1 :, :]
    tail_row = jnp.exp(last - decay_row) * weight_row * scale
    tail_col = jnp.sum(jnp.where(eye, tail_row, 0.0), axis=1, keepdims=True)
    weighted = k_ref[...].astype(F32) * tail_col
    scaled_ref[...] = weighted.astype(BF)
    tail_ref[...] = jnp.sum(weighted, axis=0, keepdims=True)
    lane = lax.broadcasted_iota(jnp.int32, (window, LANES), 1)
    aux_ref[...] = jnp.where(
        lane == 0, jnp.exp(decay_col), jnp.where(lane == 1, inner, jnp.where(lane == 2, live_col, jnp.exp(last)))
    )


def grad_kernel(norm_ref, q_ref, cot_ref, low_ref, aux_ref, tail_ref, vg_ref, live_ref, new_ref):
    norm = norm_ref[...]
    dot = jnp.sum(q_ref[...].astype(F32) * norm, axis=1, keepdims=True)
    inner = aux_ref[:, 0:1] * dot + aux_ref[:, 1:2]
    live = aux_ref[:, 2:3] / jnp.maximum(jnp.abs(inner), 1.0)
    scaled = (cot_ref[...].astype(F32) * live).astype(BF)
    vg_ref[...] = contract(low_ref[...], scaled, 0, 0).astype(BF)
    live_ref[...] = jnp.broadcast_to(live, live_ref.shape)
    new_ref[...] = aux_ref[0:1, 3:4] * norm + tail_ref[...]


def weight_kernel(own_ref, *refs):
    *f_refs, vg_ref, mine_ref, theirs_ref = refs
    width = f_refs[0].shape[1]
    rows, cols = mine_ref.shape[1:]
    count = width // (2 * rows)
    core = own_ref[2]
    for step, f_ref in enumerate(f_refs):
        part = contract(f_ref[...], vg_ref[...], 0, 0).reshape(count, 2, rows, cols)
        at = pl.ds(count * lax.rem(own_ref[3] + step, len(f_refs)), count)

        @pl.when(core == 0)
        def _():
            mine_ref[at] = part[:, 0]
            theirs_ref[at] = part[:, 1].astype(BF)

        @pl.when(core == 1)
        def _():
            mine_ref[at] = part[:, 1]
            theirs_ref[at] = part[:, 0].astype(BF)


def join_kernel(own_ref, mine_ref, theirs_ref, out_ref):
    side = out_ref.shape[0]
    core = own_ref[2]
    for y in range(side):
        at = slice(side * y, side * (y + 1))
        total = (mine_ref[at] + theirs_ref[at].astype(F32)).astype(BF)

        @pl.when(core == 0)
        def _():
            out_ref[y] = total

        @pl.when(core == 1)
        def _():
            out_ref[:, y] = total


def part_kernel(got_ref, part_ref):
    part_ref[...] = jnp.sum(got_ref[...].astype(F32), axis=0).astype(part_ref.dtype)


def value_kernel(own_ref, *refs):
    *f_refs, mine_ref, theirs_ref, v_ref, w_ref = refs
    width = f_refs[0].shape[1]
    rows, cols = w_ref.shape[2:]
    count = width // (2 * rows)
    core = own_ref[2]
    for i in range(cols // LANES):
        at = slice(LANES * i, LANES * (i + 1))
        w_ref[:, core, :, at] = mine_ref[:, 2 + i]
        w_ref[:, 1 - core, :, at] = theirs_ref[:, 2 + i]
    total = None
    for step, f_ref in enumerate(f_refs):
        at = pl.ds(count * lax.rem(own_ref[3] + step, len(f_refs)), count)
        part = contract(f_ref[...], w_ref[at].reshape(width, cols), 1, 0)
        total = part if total is None else total + part
    v_ref[...] = total.astype(BF)


def final_kernel(own_ref, mine_ref, theirs_ref, q_ref, low_ref, v_ref, scaled_ref, aux_ref, live_ref, hidden_ref, new_ref, c_ref):
    half, _, rows, _ = c_ref.shape
    cols = q_ref.shape[1] // LANES
    core = own_ref[2]
    c_ref[:, core] = mine_ref[:, core]
    c_ref[:, 1 - core] = theirs_ref[:, core]
    keep = aux_ref[0:1, 3:4]
    carried = aux_ref[:, 0:1]
    live = live_ref[:, 0:1]
    for i in range(cols):
        at = slice(LANES * i, LANES * (i + 1))
        block = c_ref[...].reshape(2 * half // cols, cols, rows, LANES)[:, i].reshape(-1, LANES)
        v = v_ref[:, at]
        numer = carried * contract(q_ref[...], block, 1, 0) + contract(low_ref[...], v, 1, 0)
        hidden_ref[:, at] = (numer * live).astype(BF)
        new_ref[:, at] = keep * block.astype(F32) + contract(scaled_ref[...], v, 0, 0)


def on_device(
    stream_map,
    lengths,
    features,
    query_rows,
    key_rows,
    log_forget,
    in_gate,
    value_weight,
    state,
    norm_state,
    cotangent,
):
    slots = lax.axis_size("dp")
    heads = lax.axis_size("mp")
    half = slots // 2
    window, head = query_rows.shape[1:]
    width = features.shape[2]
    rows = value_weight.shape[0]
    block = head * head // (slots * LANES)
    lane_groups = head // LANES
    groups = slots // lane_groups
    pairs = [(i, i ^ 1) for i in range(slots)]
    same_core = [list(range(c, slots, 2)) for c in range(2)]
    side = math.isqrt(half)
    along_y = [[[2 * (side * y + z) + c for y in range(side)] for z in range(side)] for c in range(2)]
    along_z = [[[2 * (side * y + z) + c for z in range(side)] for y in range(side)] for c in range(2)]
    first, second = along_y[0] + along_z[1], along_z[0] + along_y[1]
    q, k, cot = query_rows[0], key_rows[0], cotangent[0]
    here = lax.axis_index("dp").astype(jnp.int32)
    head_here = lax.axis_index("mp").astype(jnp.int32)
    own = jnp.stack([here, lengths[0], here & 1, head_here])

    def exchange(x, index_groups=None):
        return lax.all_to_all(x, "dp", 0, 0, axis_index_groups=index_groups, tiled=True)

    packed = pl.pallas_call(
        pack_kernel,
        grid=(lane_groups,),
        out_shape=shape((groups, lane_groups, block + 8, LANES), BF),
        in_specs=[pl.BlockSpec((head, LANES), lambda i: (0, i)), pl.BlockSpec((1, head), lambda i: (0, 0))],
        out_specs=pl.BlockSpec((groups, 1, block + 8, LANES), lambda i: (0, i, 0, 0)),
        name="pack",
        compiler_params=pltpu.CompilerParams(vmem_limit_bytes=56 << 20),
        cost_estimate=pl.CostEstimate(flops=10**6, bytes_accessed=2 << 20, transcendentals=0),
    )(state[0, 0], norm_state[0]).reshape(slots, block + 8, LANES)
    spread = exchange(packed)
    feature_parts = [features[0]] + [
        lax.ppermute(features[0], "mp", [((j + step) % heads, j) for j in range(heads)])
        for step in range(1, heads)
    ]

    low, key_scaled, aux, tail = call(
        mix_kernel,
        (
            shape((window, window), BF),
            shape((window, head), BF),
            shape((window, LANES), F32),
            shape((1, head), F32),
        ),
        [SM, VM, VM, VM, VM],
        2 * window * window * head,
    )(own, log_forget[0].reshape(1, window), in_gate[0].reshape(1, window), q, k)

    picked, norm = call(
        permute_kernel,
        (shape((half, 2 + lane_groups, block, LANES), BF), shape((1, head), F32)),
        [SM, SM, VM, VM],
        10**6,
    )(stream_map, own, spread, value_weight)
    returned = exchange(picked, same_core)

    value_grad, live, new_norm = call(
        grad_kernel,
        (shape((window, head), BF), shape((window, LANES), F32), shape((1, head), F32)),
        [VM] * 6,
        2 * window * window * head,
    )(norm, q, cot, low, aux, tail)
    mine, theirs = call(
        weight_kernel,
        (shape((half, rows, head), F32), shape((half, rows, head), BF)),
        [SM] + [VM] * (heads + 1),
        2 * window * heads * width * head,
    )(own, *feature_parts, value_grad)
    joined = call(join_kernel, shape((side, side, rows, head), BF), [SM, VM, VM], 10**6)(
        own, mine, lax.ppermute(theirs, "dp", pairs)
    )
    part = call(part_kernel, shape((side, rows, head), BF), [VM], 10**6)(exchange(joined, first))
    weight_grad = call(part_kernel, shape((rows, head), F32), [VM], 10**5)(exchange(part, second))
    swapped = lax.ppermute(returned, "dp", pairs)
    values = call(
        value_kernel,
        shape((window, head), BF),
        [SM] + [VM] * (heads + 2),
        2 * window * heads * width * head,
        [pltpu.VMEM((half, 2, rows, head), BF)],
    )(own, *feature_parts, returned, swapped)
    hidden, new_state = call(
        final_kernel,
        (shape((window, head), BF), shape((head, head), F32)),
        [SM] + [VM] * 8,
        2 * window * head * (2 * head + window),
        [pltpu.VMEM((half, 2, block, LANES), BF)],
    )(own, returned, swapped, q, low, values, key_scaled, aux, live)
    return (hidden[None], new_state[None, None], new_norm[None], weight_grad)


def solution(mesh):
    return jax.shard_map(
        on_device,
        mesh=mesh,
        in_specs=(
            P(),
            P("dp"),
            P("dp", None, "mp"),
            P("dp", None, "mp"),
            P("dp", None, "mp"),
            P("dp", None, "mp"),
            P("dp", None, "mp"),
            P("dp", "mp"),
            P("dp", "mp", None, None),
            P("dp", "mp", None),
            P("dp", None, "mp"),
        ),
        out_specs=(
            P("dp", None, "mp"),
            P("dp", "mp", None, None),
            P("dp", "mp", None),
            P("dp", "mp"),
        ),
        check_vma=False,
    )
```

```python
import math

import jax
import jax.numpy as jnp
from jax import lax
from jax.experimental import pallas as pl
from jax.experimental.pallas import tpu as pltpu
from jax.sharding import PartitionSpec as P


BF = jnp.bfloat16
F32 = jnp.float32
LANES = 128
WIDE = 56 << 20
VM = pl.BlockSpec(memory_space=pltpu.VMEM)
SM = pl.BlockSpec(memory_space=pltpu.SMEM)


def call(kernel, out, specs, flops, scratch=(), grant=16 << 20):
    moved = sum(o.size * o.dtype.itemsize for o in jax.tree.leaves(out))
    return pl.pallas_call(
        kernel,
        out_shape=out,
        in_specs=specs,
        out_specs=jax.tree.map(lambda _: VM, out),
        scratch_shapes=list(scratch),
        compiler_params=pltpu.CompilerParams(vmem_limit_bytes=grant),
        cost_estimate=pl.CostEstimate(
            flops=flops, bytes_accessed=2 * moved, transcendentals=0
        ),
    )


def shape(dims, dtype):
    return jax.ShapeDtypeStruct(tuple(dims), dtype)


def contract(a, b, da, db):
    return lax.dot_general(
        a, b, (((da,), (db,)), ((), ())), preferred_element_type=F32
    )


def pack_kernel(state_ref, norm_ref, out_ref):
    groups, cols, rows, _ = out_ref.shape
    rows -= 8
    norm = norm_ref[...]
    high = norm.astype(BF)
    low = (norm - high.astype(F32)).astype(BF)
    parts = [p[:, LANES * i : LANES * (i + 1)] for p in (high.astype(F32), low.astype(F32)) for i in range(4)]
    tile = jnp.concatenate(parts, axis=0).astype(BF)
    for i in range(cols):
        block = state_ref[:, LANES * i : LANES * (i + 1)].astype(BF)
        out_ref[:, i, :rows, :] = block.reshape(groups, rows, LANES)
        out_ref[:, i, rows:, :] = jnp.broadcast_to(tile[None], (groups, 8, LANES))


def permute_kernel(map_ref, own_ref, got_ref, w_ref, out_ref, norm_ref):
    half, parts, rows, _ = out_ref.shape
    side = math.isqrt(half)
    core = own_ref[2]
    tiles = parts - 2
    for k in range(tiles):
        even, odd = (w_ref[:, LANES * i : LANES * (i + 1)] for i in (k, tiles + k))
        for i in range(half):
            z_odd, y_odd = i % 2, i // side % 2
            if z_odd == y_odd:
                tile = odd if z_odd else even
            else:
                tile = jnp.where(core == z_odd, even, odd)
            out_ref[i, 2 + k] = tile
    own = own_ref[0]

    def body(s, source):
        slot = map_ref[s]
        out_ref[lax.shift_right_logical(slot, 1), slot & 1] = got_ref[s, :rows, :]
        return jnp.where(slot == own, s, source)

    source = lax.fori_loop(0, 2 * half, body, jnp.int32(0), unroll=8)
    tile = got_ref[source, rows:, :].astype(F32)
    total = tile[:4] + tile[4:]
    norm_ref[...] = jnp.concatenate([total[i : i + 1] for i in range(4)], axis=1)


def mix_kernel(own_ref, forget_ref, gate_ref, q_ref, k_ref, low_ref, scaled_ref, aux_ref, tail_ref):
    window = q_ref.shape[0]
    scale = q_ref.shape[1] ** (-0.5)
    length = own_ref[1]
    t = lax.broadcasted_iota(jnp.int32, (window, window), 0)
    s = lax.broadcasted_iota(jnp.int32, (window, window), 1)
    live_row = (lax.broadcasted_iota(jnp.int32, (1, window), 1) < length).astype(F32)
    live_col = (lax.broadcasted_iota(jnp.int32, (window, 1), 0) < length).astype(F32)
    causal = s <= t
    eye = s == t
    forget = forget_ref[...] * live_row
    decay_col = jnp.sum(jnp.where(causal, forget, 0.0), axis=1, keepdims=True)
    decay_row = jnp.sum(jnp.where(eye, decay_col, 0.0), axis=0, keepdims=True)
    weight_row = jnp.exp(gate_ref[...]) * live_row
    mixing = jnp.exp(jnp.where(causal, decay_col - decay_row, -1e30)) * weight_row
    combined = mixing * (contract(q_ref[...], k_ref[...], 1, 1) * scale)
    low_ref[...] = combined.astype(BF)
    inner = jnp.sum(combined, axis=1, keepdims=True)
    last = decay_col[window - 1 :, :]
    tail_row = jnp.exp(last - decay_row) * weight_row * scale
    tail_col = jnp.sum(jnp.where(eye, tail_row, 0.0), axis=1, keepdims=True)
    weighted = k_ref[...].astype(F32) * tail_col
    scaled_ref[...] = weighted.astype(BF)
    tail_ref[...] = jnp.sum(weighted, axis=0, keepdims=True)
    lane = lax.broadcasted_iota(jnp.int32, (window, LANES), 1)
    aux_ref[...] = jnp.where(
        lane == 0, jnp.exp(decay_col), jnp.where(lane == 1, inner, jnp.where(lane == 2, live_col, jnp.exp(last)))
    )


def grad_kernel(norm_ref, q_ref, cot_ref, low_ref, aux_ref, tail_ref, vg_ref, live_ref, new_ref):
    norm = norm_ref[...]
    dot = jnp.sum(q_ref[...].astype(F32) * norm, axis=1, keepdims=True)
    inner = aux_ref[:, 0:1] * dot + aux_ref[:, 1:2]
    live = aux_ref[:, 2:3] / jnp.maximum(jnp.abs(inner), 1.0)
    scaled = (cot_ref[...].astype(F32) * live).astype(BF)
    vg_ref[...] = contract(low_ref[...], scaled, 0, 0).astype(BF)
    live_ref[...] = jnp.broadcast_to(live, live_ref.shape)
    new_ref[...] = aux_ref[0:1, 3:4] * norm + tail_ref[...]


def weight_kernel(own_ref, *refs):
    *f_refs, vg_ref, mine_ref, theirs_ref = refs
    width = f_refs[0].shape[1]
    rows, cols = mine_ref.shape[1:]
    count = width // (2 * rows)
    core = own_ref[2]
    for step, f_ref in enumerate(f_refs):
        part = contract(f_ref[...], vg_ref[...], 0, 0).reshape(count, 2, rows, cols)
        at = pl.ds(count * lax.rem(own_ref[3] + step, len(f_refs)), count)

        @pl.when(core == 0)
        def _():
            mine_ref[at] = part[:, 0]
            theirs_ref[at] = part[:, 1].astype(BF)

        @pl.when(core == 1)
        def _():
            mine_ref[at] = part[:, 1]
            theirs_ref[at] = part[:, 0].astype(BF)


def join_kernel(own_ref, mine_ref, theirs_ref, out_ref):
    side = out_ref.shape[0]
    core = own_ref[2]
    for y in range(side):
        at = slice(side * y, side * (y + 1))
        total = (mine_ref[at] + theirs_ref[at].astype(F32)).astype(BF)

        @pl.when(core == 0)
        def _():
            out_ref[y] = total

        @pl.when(core == 1)
        def _():
            out_ref[:, y] = total


def part_kernel(got_ref, part_ref):
    part_ref[...] = jnp.sum(got_ref[...].astype(F32), axis=0).astype(part_ref.dtype)


def value_kernel(own_ref, *refs):
    *f_refs, mine_ref, theirs_ref, near_ref, far_ref, v_ref, w_ref = refs
    width = f_refs[0].shape[1]
    rows, cols = w_ref.shape[2:]
    count = width // (2 * rows)
    core = own_ref[2]
    tiles = near_ref.shape[1]
    for odd in range(2):
        for i in range(tiles):
            at = slice(LANES * (tiles * odd + i), LANES * (tiles * odd + i + 1))
            other = slice(LANES * (tiles * (1 - odd) + i), LANES * (tiles * (1 - odd) + i + 1))

            @pl.when(own_ref[4] == odd)
            def _():
                w_ref[:, core, :, at] = mine_ref[:, 2 + i]
                w_ref[:, core, :, other] = near_ref[:, i]

            @pl.when(own_ref[5] == odd)
            def _():
                w_ref[:, 1 - core, :, at] = theirs_ref[:, 2 + i]
                w_ref[:, 1 - core, :, other] = far_ref[:, i]

    total = None
    for step, f_ref in enumerate(f_refs):
        at = pl.ds(count * lax.rem(own_ref[3] + step, len(f_refs)), count)
        part = contract(f_ref[...], w_ref[at].reshape(width, cols), 1, 0)
        total = part if total is None else total + part
    v_ref[...] = total.astype(BF)


def final_kernel(own_ref, mine_ref, theirs_ref, q_ref, low_ref, v_ref, scaled_ref, aux_ref, live_ref, hidden_ref, new_ref, c_ref):
    half, _, rows, _ = c_ref.shape
    cols = q_ref.shape[1] // LANES
    core = own_ref[2]
    c_ref[:, core] = mine_ref[:, core]
    c_ref[:, 1 - core] = theirs_ref[:, core]
    keep = aux_ref[0:1, 3:4]
    carried = aux_ref[:, 0:1]
    live = live_ref[:, 0:1]
    for i in range(cols):
        at = slice(LANES * i, LANES * (i + 1))
        block = c_ref[...].reshape(2 * half // cols, cols, rows, LANES)[:, i].reshape(-1, LANES)
        v = v_ref[:, at]
        numer = carried * contract(q_ref[...], block, 1, 0) + contract(low_ref[...], v, 1, 0)
        hidden_ref[:, at] = (numer * live).astype(BF)
        new_ref[:, at] = keep * block.astype(F32) + contract(scaled_ref[...], v, 0, 0)


def on_device(
    stream_map,
    lengths,
    features,
    query_rows,
    key_rows,
    log_forget,
    in_gate,
    value_weight,
    state,
    norm_state,
    cotangent,
):
    slots = lax.axis_size("dp")
    heads = lax.axis_size("mp")
    half = slots // 2
    window, head = query_rows.shape[1:]
    width = features.shape[2]
    rows = value_weight.shape[0]
    block = head * head // (slots * LANES)
    lane_groups = head // LANES
    groups = slots // lane_groups
    pairs = [(i, i ^ 1) for i in range(slots)]
    same_core = [list(range(c, slots, 2)) for c in range(2)]
    side = math.isqrt(half)
    along_y = [[[2 * (side * y + z) + c for y in range(side)] for z in range(side)] for c in range(2)]
    along_z = [[[2 * (side * y + z) + c for z in range(side)] for y in range(side)] for c in range(2)]
    every = [(y, z, c) for y in range(side) for z in range(side) for c in range(2)]
    near = [(2 * (side * y + z) + c, 2 * (side * (y ^ c) + (z ^ (1 - c))) + c) for y, z, c in every]
    first, second = along_y[0] + along_z[1], along_z[0] + along_y[1]
    q, k, cot = query_rows[0], key_rows[0], cotangent[0]
    here = lax.axis_index("dp").astype(jnp.int32)
    head_here = lax.axis_index("mp").astype(jnp.int32)
    core = here & 1
    bits = side.bit_length() - 1
    odd_z, odd_y = lax.shift_right_logical(here, 1) & 1, lax.shift_right_logical(here, 1 + bits) & 1
    odds = [jnp.where(core == 0, odd_z, odd_y), jnp.where(core == 0, odd_y, odd_z)]
    own = jnp.stack([here, lengths[0], core, head_here, *odds])

    def exchange(x, index_groups=None):
        return lax.all_to_all(x, "dp", 0, 0, axis_index_groups=index_groups, tiled=True)

    packed = call(
        pack_kernel, shape((groups, lane_groups, block + 8, LANES), BF), [VM, VM], 10**6, grant=WIDE
    )(state[0, 0], norm_state[0]).reshape(slots, block + 8, LANES)
    spread = exchange(packed)
    feature_parts = [features[0]] + [
        lax.ppermute(features[0], "mp", [((j + step) % heads, j) for j in range(heads)])
        for step in range(1, heads)
    ]

    low, key_scaled, aux, tail = call(
        mix_kernel,
        (
            shape((window, window), BF),
            shape((window, head), BF),
            shape((window, LANES), F32),
            shape((1, head), F32),
        ),
        [SM, VM, VM, VM, VM],
        2 * window * window * head,
    )(own, log_forget[0].reshape(1, window), in_gate[0].reshape(1, window), q, k)

    picked, norm = call(
        permute_kernel,
        (shape((half, 2 + lane_groups // 2, block, LANES), BF), shape((1, head), F32)),
        [SM, SM, VM, VM],
        10**6,
    )(stream_map, own, spread, value_weight)
    returned = exchange(picked, same_core)

    value_grad, live, new_norm = call(
        grad_kernel,
        (shape((window, head), BF), shape((window, LANES), F32), shape((1, head), F32)),
        [VM] * 6,
        2 * window * window * head,
    )(norm, q, cot, low, aux, tail)
    mine, theirs = call(
        weight_kernel,
        (shape((half, rows, head), F32), shape((half, rows, head), BF)),
        [SM] + [VM] * (heads + 1),
        2 * window * heads * width * head,
    )(own, *feature_parts, value_grad)
    joined = call(join_kernel, shape((side, side, rows, head), BF), [SM, VM, VM], 10**6)(
        own, mine, lax.ppermute(theirs, "dp", pairs)
    )
    part = call(part_kernel, shape((side, rows, head), BF), [VM], 10**6)(exchange(joined, first))
    weight_grad = call(part_kernel, shape((rows, head), F32), [VM], 10**5)(exchange(part, second))
    weight_near = lax.ppermute(returned[:, 2:], "dp", near)
    swapped = lax.ppermute(returned, "dp", pairs)
    weight_far = lax.ppermute(weight_near, "dp", pairs)
    values = call(
        value_kernel,
        shape((window, head), BF),
        [SM] + [VM] * (heads + 4),
        2 * window * heads * width * head,
        [pltpu.VMEM((half, 2, rows, head), BF)],
        WIDE,
    )(own, *feature_parts, returned, swapped, weight_near, weight_far)
    hidden, new_state = call(
        final_kernel,
        (shape((window, head), BF), shape((head, head), F32)),
        [SM] + [VM] * 8,
        2 * window * head * (2 * head + window),
        [pltpu.VMEM((half, 2, block, LANES), BF)],
        WIDE,
    )(own, returned, swapped, q, low, values, key_scaled, aux, live)
    return (hidden[None], new_state[None, None], new_norm[None], weight_grad)


def solution(mesh):
    return jax.shard_map(
        on_device,
        mesh=mesh,
        in_specs=(
            P(),
            P("dp"),
            P("dp", None, "mp"),
            P("dp", None, "mp"),
            P("dp", None, "mp"),
            P("dp", None, "mp"),
            P("dp", None, "mp"),
            P("dp", "mp"),
            P("dp", "mp", None, None),
            P("dp", "mp", None),
            P("dp", None, "mp"),
        ),
        out_specs=(
            P("dp", None, "mp"),
            P("dp", "mp", None, None),
            P("dp", "mp", None),
            P("dp", "mp"),
        ),
        check_vma=False,
    )
```

```python
import functools

import functools
import math

import jax
import jax.numpy as jnp
from jax import lax
from jax.experimental import pallas as pl
from jax.experimental.pallas import tpu as pltpu
from jax.sharding import PartitionSpec as P


BF = jnp.bfloat16
F32 = jnp.float32
LANES = 128
WIDE = 56 << 20
VM = pl.BlockSpec(memory_space=pltpu.VMEM)
SM = pl.BlockSpec(memory_space=pltpu.SMEM)


def call(kernel, out, specs, flops, scratch=(), grant=16 << 20):
    moved = sum(o.size * o.dtype.itemsize for o in jax.tree.leaves(out))
    return pl.pallas_call(
        kernel,
        out_shape=out,
        in_specs=specs,
        out_specs=jax.tree.map(lambda _: VM, out),
        scratch_shapes=list(scratch),
        compiler_params=pltpu.CompilerParams(vmem_limit_bytes=grant),
        cost_estimate=pl.CostEstimate(
            flops=flops, bytes_accessed=2 * moved, transcendentals=0
        ),
    )


def shape(dims, dtype):
    return jax.ShapeDtypeStruct(tuple(dims), dtype)


def contract(a, b, da, db):
    return lax.dot_general(
        a, b, (((da,), (db,)), ((), ())), preferred_element_type=F32
    )


def pack_kernel(state_ref, norm_ref, out_ref):
    groups, cols, rows, _ = out_ref.shape
    rows -= 8
    norm = norm_ref[...]
    high = norm.astype(BF)
    low = (norm - high.astype(F32)).astype(BF)
    parts = [p[:, LANES * i : LANES * (i + 1)] for p in (high.astype(F32), low.astype(F32)) for i in range(4)]
    tile = jnp.concatenate(parts, axis=0).astype(BF)
    for i in range(cols):
        block = state_ref[:, LANES * i : LANES * (i + 1)].astype(BF)
        out_ref[:, i, :rows, :] = block.reshape(groups, rows, LANES)
        out_ref[:, i, rows:, :] = jnp.broadcast_to(tile[None], (groups, 8, LANES))


def permute_kernel(map_ref, own_ref, got_ref, w_ref, out_ref, norm_ref):
    half, parts, rows, _ = out_ref.shape
    side = math.isqrt(half)
    tiles = parts - 2
    for k in range(tiles):
        even, odd = (w_ref[:, LANES * i : LANES * (i + 1)] for i in (k, tiles + k))
        for i in range(half):
            tile = odd if (i % 2) ^ (i // side % 2) else even
            out_ref[i, 2 + k] = tile
    own = own_ref[0]

    def body(s, source):
        slot = map_ref[s]
        out_ref[lax.shift_right_logical(slot, 1), slot & 1] = got_ref[s, :rows, :]
        return jnp.where(slot == own, s, source)

    source = lax.fori_loop(0, 2 * half, body, jnp.int32(0), unroll=8)
    tile = got_ref[source, rows:, :].astype(F32)
    total = tile[:4] + tile[4:]
    norm_ref[...] = jnp.concatenate([total[i : i + 1] for i in range(4)], axis=1)


def mix_kernel(own_ref, forget_ref, gate_ref, q_ref, k_ref, low_ref, scaled_ref, aux_ref, tail_ref):
    window = q_ref.shape[0]
    scale = q_ref.shape[1] ** (-0.5)
    length = own_ref[1]
    t = lax.broadcasted_iota(jnp.int32, (window, window), 0)
    s = lax.broadcasted_iota(jnp.int32, (window, window), 1)
    live_row = (lax.broadcasted_iota(jnp.int32, (1, window), 1) < length).astype(F32)
    live_col = (lax.broadcasted_iota(jnp.int32, (window, 1), 0) < length).astype(F32)
    causal = s <= t
    eye = s == t
    forget = forget_ref[...] * live_row
    decay_col = jnp.sum(jnp.where(causal, forget, 0.0), axis=1, keepdims=True)
    decay_row = jnp.sum(jnp.where(eye, decay_col, 0.0), axis=0, keepdims=True)
    weight_row = jnp.exp(gate_ref[...]) * live_row
    mixing = jnp.exp(jnp.where(causal, decay_col - decay_row, -1e30)) * weight_row
    combined = mixing * (contract(q_ref[...], k_ref[...], 1, 1) * scale)
    low_ref[...] = combined.astype(BF)
    inner = jnp.sum(combined, axis=1, keepdims=True)
    last = decay_col[window - 1 :, :]
    tail_row = jnp.exp(last - decay_row) * weight_row * scale
    tail_col = jnp.sum(jnp.where(eye, tail_row, 0.0), axis=1, keepdims=True)
    weighted = k_ref[...].astype(F32) * tail_col
    scaled_ref[...] = weighted.astype(BF)
    tail_ref[...] = jnp.sum(weighted, axis=0, keepdims=True)
    lane = lax.broadcasted_iota(jnp.int32, (window, LANES), 1)
    aux_ref[...] = jnp.where(
        lane == 0, jnp.exp(decay_col), jnp.where(lane == 1, inner, jnp.where(lane == 2, live_col, jnp.exp(last)))
    )


def grad_kernel(norm_ref, q_ref, cot_ref, low_ref, aux_ref, tail_ref, vg_ref, live_ref, new_ref):
    norm = norm_ref[...]
    dot = jnp.sum(q_ref[...].astype(F32) * norm, axis=1, keepdims=True)
    inner = aux_ref[:, 0:1] * dot + aux_ref[:, 1:2]
    live = aux_ref[:, 2:3] / jnp.maximum(jnp.abs(inner), 1.0)
    scaled = (cot_ref[...].astype(F32) * live).astype(BF)
    vg_ref[...] = contract(low_ref[...], scaled, 0, 0).astype(BF)
    live_ref[...] = jnp.broadcast_to(live, live_ref.shape)
    new_ref[...] = aux_ref[0:1, 3:4] * norm + tail_ref[...]


def weight_kernel(own_ref, *refs):
    *f_refs, vg_ref, mine_ref, theirs_ref = refs
    width = f_refs[0].shape[1]
    rows, cols = mine_ref.shape[1:]
    count = width // (2 * rows)
    core = own_ref[2]
    for step, f_ref in enumerate(f_refs):
        part = contract(f_ref[...], vg_ref[...], 0, 0).reshape(count, 2, rows, cols)
        at = pl.ds(count * lax.rem(own_ref[3] + step, len(f_refs)), count)

        @pl.when(core == 0)
        def _():
            mine_ref[at] = part[:, 0]
            theirs_ref[at] = part[:, 1].astype(BF)

        @pl.when(core == 1)
        def _():
            mine_ref[at] = part[:, 1]
            theirs_ref[at] = part[:, 0].astype(BF)


def join_kernel(own_ref, mine_ref, theirs_ref, out_ref):
    side = out_ref.shape[0]
    core = own_ref[2]
    for y in range(side):
        at = slice(side * y, side * (y + 1))
        total = (mine_ref[at] + theirs_ref[at].astype(F32)).astype(BF)

        @pl.when(core == 0)
        def _():
            out_ref[y] = total

        @pl.when(core == 1)
        def _():
            out_ref[:, y] = total


def part_kernel(got_ref, part_ref):
    part_ref[...] = jnp.sum(got_ref[...].astype(F32), axis=0).astype(part_ref.dtype)


def half_kernel(heads, flip, own_ref, *refs):
    f_refs = refs[:heads]
    w_mine_ref, w_theirs_ref, mine_ref, theirs_ref, q_ref, low_ref, scaled_ref, aux_ref, live_ref = refs[heads : heads + 9]
    hidden_ref, new_ref, w_ref, c_ref = refs[-4:]
    width = f_refs[0].shape[1]
    half, _, rows, cols = w_ref.shape
    count = width // (2 * rows)
    core, odd = own_ref[2], own_ref[4] ^ flip
    for i in range(cols // LANES):
        at = slice(LANES * i, LANES * (i + 1))
        part = i + w_mine_ref.shape[2] - cols // LANES
        w_ref[:, core, :, at] = w_mine_ref[:, :, part].reshape(half, rows, LANES)
        w_ref[:, 1 - core, :, at] = w_theirs_ref[:, :, part].reshape(half, rows, LANES)
    c_ref[core] = mine_ref[:, odd, core]
    c_ref[1 - core] = theirs_ref[:, odd, core]
    memory = jnp.concatenate([c_ref[i].reshape(-1, LANES) for i in range(2)], axis=1)
    total = None
    for step, f_ref in enumerate(f_refs):
        at = pl.ds(count * lax.rem(own_ref[3] + step, heads), count)
        part = contract(f_ref[...], w_ref[at].reshape(width, cols), 1, 0)
        total = part if total is None else total + part
    values = total.astype(BF)
    numer = aux_ref[:, 0:1] * contract(q_ref[...], memory, 1, 0) + contract(low_ref[...], values, 1, 0)
    hidden_ref[...] = (numer * live_ref[:, 0:1]).astype(BF)
    new_ref[...] = aux_ref[0:1, 3:4] * memory.astype(F32) + contract(scaled_ref[...], values, 0, 0)


def on_device(
    stream_map,
    lengths,
    features,
    query_rows,
    key_rows,
    log_forget,
    in_gate,
    value_weight,
    state,
    norm_state,
    cotangent,
):
    slots = lax.axis_size("dp")
    heads = lax.axis_size("mp")
    half = slots // 2
    window, head = query_rows.shape[1:]
    width = features.shape[2]
    rows = value_weight.shape[0]
    block = head * head // (slots * LANES)
    lane_groups = head // LANES
    groups = slots // lane_groups
    pairs = [(i, i ^ 1) for i in range(slots)]
    same_core = [list(range(c, slots, 2)) for c in range(2)]
    side = math.isqrt(half)
    along_y = [[[2 * (side * y + z) + c for y in range(side)] for z in range(side)] for c in range(2)]
    along_z = [[[2 * (side * y + z) + c for z in range(side)] for y in range(side)] for c in range(2)]
    every = [(y, z, c) for y in range(side) for z in range(side) for c in range(2)]
    near = [(2 * (side * y + z) + c, 2 * (side * (y ^ c) + (z ^ (1 - c))) + c) for y, z, c in every]
    first, second = along_y[0] + along_z[1], along_z[0] + along_y[1]
    q, k, cot = query_rows[0], key_rows[0], cotangent[0]
    here = lax.axis_index("dp").astype(jnp.int32)
    head_here = lax.axis_index("mp").astype(jnp.int32)
    core = here & 1
    bits = side.bit_length() - 1
    odd_z, odd_y = lax.shift_right_logical(here, 1) & 1, lax.shift_right_logical(here, 1 + bits) & 1
    own = jnp.stack([here, lengths[0], core, head_here, odd_y ^ odd_z])

    def exchange(x, index_groups=None):
        return lax.all_to_all(x, "dp", 0, 0, axis_index_groups=index_groups, tiled=True)

    packed = call(
        pack_kernel, shape((groups, lane_groups, block + 8, LANES), BF), [VM, VM], 10**6, grant=WIDE
    )(state[0, 0], norm_state[0]).reshape(slots, block + 8, LANES)
    spread = exchange(packed)
    feature_parts = [features[0]] + [
        lax.ppermute(features[0], "mp", [((j + step) % heads, j) for j in range(heads)])
        for step in range(1, heads)
    ]

    low, key_scaled, aux, tail = call(
        mix_kernel,
        (
            shape((window, window), BF),
            shape((window, head), BF),
            shape((window, LANES), F32),
            shape((1, head), F32),
        ),
        [SM, VM, VM, VM, VM],
        2 * window * window * head,
    )(own, log_forget[0].reshape(1, window), in_gate[0].reshape(1, window), q, k)

    picked, norm = call(
        permute_kernel,
        (shape((half, 2 + lane_groups // 2, block, LANES), BF), shape((1, head), F32)),
        [SM, SM, VM, VM],
        10**6,
    )(stream_map, own, spread, value_weight)
    returned = exchange(picked, same_core)

    value_grad, live, new_norm = call(
        grad_kernel,
        (shape((window, head), BF), shape((window, LANES), F32), shape((1, head), F32)),
        [VM] * 6,
        2 * window * window * head,
    )(norm, q, cot, low, aux, tail)
    mine, theirs = call(
        weight_kernel,
        (shape((half, rows, head), F32), shape((half, rows, head), BF)),
        [SM] + [VM] * (heads + 1),
        2 * window * heads * width * head,
    )(own, *feature_parts, value_grad)
    joined = call(join_kernel, shape((side, side, rows, head), BF), [SM, VM, VM], 10**6)(
        own, mine, lax.ppermute(theirs, "dp", pairs)
    )
    part = call(part_kernel, shape((side, rows, head), BF), [VM], 10**6)(exchange(joined, first))
    weight_grad = call(part_kernel, shape((rows, head), F32), [VM], 10**5)(exchange(part, second))
    weight_near = lax.ppermute(returned[:, 2:], "dp", near)
    swapped = lax.ppermute(returned, "dp", pairs)
    weight_far = lax.ppermute(weight_near, "dp", pairs)

    def by_pairs(x):
        return x.reshape(half // 2, 2, *x.shape[1:])

    def column_half(flip, w_mine, w_theirs, *previous):
        def out_map(i, own):
            return 0, own[4] ^ flip

        out = (shape((window, head), BF), shape((head, head), F32))
        operands = [*feature_parts, by_pairs(w_mine), by_pairs(w_theirs), by_pairs(returned), by_pairs(swapped)]
        operands += [q, low, key_scaled, aux, live]
        return pl.pallas_call(
            functools.partial(half_kernel, heads, flip),
            out_shape=out,
            grid_spec=pltpu.PrefetchScalarGridSpec(
                num_scalar_prefetch=1,
                grid=(1,),
                in_specs=[VM] * len(operands) + [pl.BlockSpec(memory_space=pl.ANY)] * len(previous),
                out_specs=tuple(pl.BlockSpec((o.shape[0], head // 2), out_map) for o in out),
                scratch_shapes=[
                    pltpu.VMEM((half, 2, rows, head // 2), BF),
                    pltpu.VMEM((2, half // 2, block, LANES), BF),
                ],
            ),
            input_output_aliases={1 + len(operands) + i: i for i in range(len(previous))},
            compiler_params=pltpu.CompilerParams(vmem_limit_bytes=WIDE),
            cost_estimate=pl.CostEstimate(
                flops=window * head * (heads * width + 2 * head + window), bytes_accessed=4 << 20, transcendentals=0
            ),
        )(own, *operands, *previous)

    early = column_half(0, returned, swapped)
    hidden, new_state = column_half(1, weight_near, weight_far, *early)
    return (hidden[None], new_state[None, None], new_norm[None], weight_grad)


def solution(mesh):
    return jax.shard_map(
        on_device,
        mesh=mesh,
        in_specs=(
            P(),
            P("dp"),
            P("dp", None, "mp"),
            P("dp", None, "mp"),
            P("dp", None, "mp"),
            P("dp", None, "mp"),
            P("dp", None, "mp"),
            P("dp", "mp"),
            P("dp", "mp", None, None),
            P("dp", "mp", None),
            P("dp", None, "mp"),
        ),
        out_specs=(
            P("dp", None, "mp"),
            P("dp", "mp", None, None),
            P("dp", "mp", None),
            P("dp", "mp"),
        ),
        check_vma=False,
    )
```

```python
import functools

import functools
import math

import jax
import jax.numpy as jnp
from jax import lax
from jax.experimental import pallas as pl
from jax.experimental.pallas import tpu as pltpu
from jax.sharding import PartitionSpec as P


BF = jnp.bfloat16
F32 = jnp.float32
LANES = 128
WIDE = 56 << 20
VM = pl.BlockSpec(memory_space=pltpu.VMEM)
SM = pl.BlockSpec(memory_space=pltpu.SMEM)


def call(kernel, out, specs, flops, scratch=(), grant=16 << 20):
    moved = sum(o.size * o.dtype.itemsize for o in jax.tree.leaves(out))
    return pl.pallas_call(
        kernel,
        out_shape=out,
        in_specs=specs,
        out_specs=jax.tree.map(lambda _: VM, out),
        scratch_shapes=list(scratch),
        compiler_params=pltpu.CompilerParams(vmem_limit_bytes=grant),
        cost_estimate=pl.CostEstimate(
            flops=flops, bytes_accessed=2 * moved, transcendentals=0
        ),
    )


def shape(dims, dtype):
    return jax.ShapeDtypeStruct(tuple(dims), dtype)


def contract(a, b, da, db):
    return lax.dot_general(
        a, b, (((da,), (db,)), ((), ())), preferred_element_type=F32
    )


def pack_kernel(state_ref, norm_ref, out_ref, whole_ref, block_ref, in_sem, out_sem):
    groups, cols, rows, _ = block_ref.shape
    rows -= 8
    pieces = in_sem.shape[0]
    some = groups // pieces
    loads = []
    for p in range(pieces):
        at = pl.ds(p * some * rows, some * rows)
        loads.append(pltpu.make_async_copy(state_ref.at[at], whole_ref.at[at], in_sem.at[p]))
        loads[p].start()
    norm = norm_ref[...]
    high = norm.astype(BF)
    low = (norm - high.astype(F32)).astype(BF)
    parts = [p[:, LANES * i : LANES * (i + 1)] for p in (high.astype(F32), low.astype(F32)) for i in range(4)]
    tile = jnp.concatenate(parts, axis=0).astype(BF)
    block_ref[:, :, rows:, :] = jnp.broadcast_to(tile[None, None], (groups, cols, 8, LANES))
    stores = []
    for p in range(pieces):
        loads[p].wait()
        to = slice(some * p, some * (p + 1))
        for i in range(cols):
            block = whole_ref[some * rows * p : some * rows * (p + 1), LANES * i : LANES * (i + 1)].astype(BF)
            block_ref[to, i, :rows, :] = block.reshape(some, rows, LANES)
        stores.append(pltpu.make_async_copy(block_ref.at[to], out_ref.at[to], out_sem.at[p]))
        stores[p].start()
    for copy in stores:
        copy.wait()


def permute_kernel(map_ref, own_ref, got_ref, w_ref, out_ref, norm_ref):
    half, parts, rows, _ = out_ref.shape
    side = math.isqrt(half)
    tiles = parts - 2
    for k in range(tiles):
        even, odd = (w_ref[:, LANES * i : LANES * (i + 1)] for i in (k, tiles + k))
        for i in range(half):
            tile = odd if (i % 2) ^ (i // side % 2) else even
            out_ref[i, 2 + k] = tile
    own = own_ref[0]

    def body(s, source):
        slot = map_ref[s]
        out_ref[lax.shift_right_logical(slot, 1), slot & 1] = got_ref[s, :rows, :]
        return jnp.where(slot == own, s, source)

    source = lax.fori_loop(0, 2 * half, body, jnp.int32(0), unroll=8)
    tile = got_ref[source, rows:, :].astype(F32)
    total = tile[:4] + tile[4:]
    norm_ref[...] = jnp.concatenate([total[i : i + 1] for i in range(4)], axis=1)


def mix_kernel(own_ref, forget_ref, gate_ref, q_ref, k_ref, low_ref, scaled_ref, aux_ref, tail_ref):
    window = q_ref.shape[0]
    scale = q_ref.shape[1] ** (-0.5)
    length = own_ref[1]
    t = lax.broadcasted_iota(jnp.int32, (window, window), 0)
    s = lax.broadcasted_iota(jnp.int32, (window, window), 1)
    live_row = (lax.broadcasted_iota(jnp.int32, (1, window), 1) < length).astype(F32)
    live_col = (lax.broadcasted_iota(jnp.int32, (window, 1), 0) < length).astype(F32)
    causal = s <= t
    eye = s == t
    forget = forget_ref[...] * live_row
    decay_col = jnp.sum(jnp.where(causal, forget, 0.0), axis=1, keepdims=True)
    decay_row = jnp.sum(jnp.where(eye, decay_col, 0.0), axis=0, keepdims=True)
    weight_row = jnp.exp(gate_ref[...]) * live_row
    mixing = jnp.exp(jnp.where(causal, decay_col - decay_row, -1e30)) * weight_row
    combined = mixing * (contract(q_ref[...], k_ref[...], 1, 1) * scale)
    low_ref[...] = combined.astype(BF)
    inner = jnp.sum(combined, axis=1, keepdims=True)
    last = decay_col[window - 1 :, :]
    tail_row = jnp.exp(last - decay_row) * weight_row * scale
    tail_col = jnp.sum(jnp.where(eye, tail_row, 0.0), axis=1, keepdims=True)
    weighted = k_ref[...].astype(F32) * tail_col
    scaled_ref[...] = weighted.astype(BF)
    tail_ref[...] = jnp.sum(weighted, axis=0, keepdims=True)
    lane = lax.broadcasted_iota(jnp.int32, (window, LANES), 1)
    aux_ref[...] = jnp.where(
        lane == 0, jnp.exp(decay_col), jnp.where(lane == 1, inner, jnp.where(lane == 2, live_col, jnp.exp(last)))
    )


def grad_kernel(norm_ref, q_ref, cot_ref, low_ref, aux_ref, tail_ref, vg_ref, live_ref, new_ref):
    norm = norm_ref[...]
    dot = jnp.sum(q_ref[...].astype(F32) * norm, axis=1, keepdims=True)
    inner = aux_ref[:, 0:1] * dot + aux_ref[:, 1:2]
    live = aux_ref[:, 2:3] / jnp.maximum(jnp.abs(inner), 1.0)
    scaled = (cot_ref[...].astype(F32) * live).astype(BF)
    vg_ref[...] = contract(low_ref[...], scaled, 0, 0).astype(BF)
    live_ref[...] = jnp.broadcast_to(live, live_ref.shape)
    new_ref[...] = aux_ref[0:1, 3:4] * norm + tail_ref[...]


def weight_kernel(own_ref, *refs):
    *f_refs, vg_ref, mine_ref, theirs_ref = refs
    width = f_refs[0].shape[1]
    rows, cols = mine_ref.shape[1:]
    count = width // (2 * rows)
    core = own_ref[2]
    for step, f_ref in enumerate(f_refs):
        part = contract(f_ref[...], vg_ref[...], 0, 0).reshape(count, 2, rows, cols)
        at = pl.ds(count * lax.rem(own_ref[3] + step, len(f_refs)), count)

        @pl.when(core == 0)
        def _():
            mine_ref[at] = part[:, 0]
            theirs_ref[at] = part[:, 1].astype(BF)

        @pl.when(core == 1)
        def _():
            mine_ref[at] = part[:, 1]
            theirs_ref[at] = part[:, 0].astype(BF)


def join_kernel(own_ref, mine_ref, theirs_ref, out_ref):
    side = out_ref.shape[0]
    core = own_ref[2]
    for y in range(side):
        at = slice(side * y, side * (y + 1))
        total = (mine_ref[at] + theirs_ref[at].astype(F32)).astype(BF)

        @pl.when(core == 0)
        def _():
            out_ref[y] = total

        @pl.when(core == 1)
        def _():
            out_ref[:, y] = total


def part_kernel(got_ref, part_ref):
    part_ref[...] = jnp.sum(got_ref[...].astype(F32), axis=0).astype(part_ref.dtype)


def half_kernel(heads, own_ref, *refs):
    f_refs = refs[:heads]
    w_mine_ref, w_theirs_ref, mine_ref, theirs_ref, q_ref, low_ref, scaled_ref, aux_ref, live_ref = refs[heads : heads + 9]
    hidden_ref, new_ref, w_ref, c_ref = refs[-4:]
    width = f_refs[0].shape[1]
    half, _, rows, cols = w_ref.shape
    count = width // (2 * rows)
    core = own_ref[2]
    for i in range(cols // LANES):
        at = slice(LANES * i, LANES * (i + 1))
        w_ref[:, core, :, at] = w_mine_ref[:, :, i].reshape(half, rows, LANES)
        w_ref[:, 1 - core, :, at] = w_theirs_ref[:, :, i].reshape(half, rows, LANES)
    c_ref[core] = mine_ref[:, 0, 0]
    c_ref[1 - core] = theirs_ref[:, 0, 0]
    memory = jnp.concatenate([c_ref[i].reshape(-1, LANES) for i in range(2)], axis=1)
    total = None
    for step, f_ref in enumerate(f_refs):
        at = pl.ds(count * lax.rem(own_ref[3] + step, heads), count)
        part = contract(f_ref[...], w_ref[at].reshape(width, cols), 1, 0)
        total = part if total is None else total + part
    values = total.astype(BF)
    numer = aux_ref[:, 0:1] * contract(q_ref[...], memory, 1, 0) + contract(low_ref[...], values, 1, 0)
    hidden_ref[...] = (numer * live_ref[:, 0:1]).astype(BF)
    new_ref[...] = aux_ref[0:1, 3:4] * memory.astype(F32) + contract(scaled_ref[...], values, 0, 0)


def on_device(
    stream_map,
    lengths,
    features,
    query_rows,
    key_rows,
    log_forget,
    in_gate,
    value_weight,
    state,
    norm_state,
    cotangent,
):
    slots = lax.axis_size("dp")
    heads = lax.axis_size("mp")
    half = slots // 2
    window, head = query_rows.shape[1:]
    width = features.shape[2]
    rows = value_weight.shape[0]
    block = head * head // (slots * LANES)
    lane_groups = head // LANES
    groups = slots // lane_groups
    pairs = [(i, i ^ 1) for i in range(slots)]
    same_core = [list(range(c, slots, 2)) for c in range(2)]
    side = math.isqrt(half)
    along_y = [[[2 * (side * y + z) + c for y in range(side)] for z in range(side)] for c in range(2)]
    along_z = [[[2 * (side * y + z) + c for z in range(side)] for y in range(side)] for c in range(2)]
    every = [(y, z, c) for y in range(side) for z in range(side) for c in range(2)]
    near = [(2 * (side * y + z) + c, 2 * (side * (y ^ c) + (z ^ (1 - c))) + c) for y, z, c in every]
    first, second = along_y[0] + along_z[1], along_z[0] + along_y[1]
    q, k, cot = query_rows[0], key_rows[0], cotangent[0]
    here = lax.axis_index("dp").astype(jnp.int32)
    head_here = lax.axis_index("mp").astype(jnp.int32)
    core = here & 1
    bits = side.bit_length() - 1
    odd_z, odd_y = lax.shift_right_logical(here, 1) & 1, lax.shift_right_logical(here, 1 + bits) & 1
    own = jnp.stack([here, lengths[0], core, head_here, odd_y ^ odd_z])

    def exchange(x, index_groups=None):
        return lax.all_to_all(x, "dp", 0, 0, axis_index_groups=index_groups, tiled=True)

    packed_shape = (groups, lane_groups, block + 8, LANES)
    pieces = min(4, groups)
    packed = pl.pallas_call(
        pack_kernel,
        out_shape=shape(packed_shape, BF),
        in_specs=[pl.BlockSpec(memory_space=pl.ANY), VM],
        out_specs=pl.BlockSpec(memory_space=pl.ANY),
        scratch_shapes=[
            pltpu.VMEM((head, head), F32),
            pltpu.VMEM(packed_shape, BF),
            pltpu.SemaphoreType.DMA((pieces,)),
            pltpu.SemaphoreType.DMA((pieces,)),
        ],
        name="pack",
        compiler_params=pltpu.CompilerParams(vmem_limit_bytes=WIDE),
        cost_estimate=pl.CostEstimate(flops=10**6, bytes_accessed=2 << 20, transcendentals=0),
    )(state[0, 0], norm_state[0]).reshape(slots, block + 8, LANES)
    spread = exchange(packed)
    feature_parts = [features[0]] + [
        lax.ppermute(features[0], "mp", [((j + step) % heads, j) for j in range(heads)])
        for step in range(1, heads)
    ]

    low, key_scaled, aux, tail = call(
        mix_kernel,
        (
            shape((window, window), BF),
            shape((window, head), BF),
            shape((window, LANES), F32),
            shape((1, head), F32),
        ),
        [SM, VM, VM, VM, VM],
        2 * window * window * head,
    )(own, log_forget[0].reshape(1, window), in_gate[0].reshape(1, window), q, k)

    picked, norm = call(
        permute_kernel,
        (shape((half, 2 + lane_groups // 2, block, LANES), BF), shape((1, head), F32)),
        [SM, SM, VM, VM],
        10**6,
    )(stream_map, own, spread, value_weight)
    returned = exchange(picked, same_core)

    value_grad, live, new_norm = call(
        grad_kernel,
        (shape((window, head), BF), shape((window, LANES), F32), shape((1, head), F32)),
        [VM] * 6,
        2 * window * window * head,
    )(norm, q, cot, low, aux, tail)
    mine, theirs = call(
        weight_kernel,
        (shape((half, rows, head), F32), shape((half, rows, head), BF)),
        [SM] + [VM] * (heads + 1),
        2 * window * heads * width * head,
    )(own, *feature_parts, value_grad)
    joined = call(join_kernel, shape((side, side, rows, head), BF), [SM, VM, VM], 10**6)(
        own, mine, lax.ppermute(theirs, "dp", pairs)
    )
    part = call(part_kernel, shape((side, rows, head), BF), [VM], 10**6)(exchange(joined, first))
    weight_grad = call(part_kernel, shape((rows, head), F32), [VM], 10**5)(exchange(part, second))
    weight_near = lax.ppermute(returned[:, 2:], "dp", near)
    swapped = lax.ppermute(returned, "dp", pairs)
    weight_far = lax.ppermute(weight_near, "dp", pairs)

    def by_pairs(x):
        return x.reshape(half // 2, 2, *x.shape[1:])

    def column_half(flip, w_mine, w_theirs, *previous):
        def out_map(i, own):
            return 0, own[4] ^ flip

        tiles = lane_groups // 2
        at_part = w_mine.shape[1] // tiles - 1
        w_spec = pl.BlockSpec((half // 2, 2, tiles, block, LANES), lambda i, own: (0, 0, at_part, 0, 0))
        c_spec = pl.BlockSpec(
            (half // 2, 1, 1, block, LANES), lambda i, own: (0, own[4] ^ flip, own[2], 0, 0)
        )
        out = (shape((window, head), BF), shape((head, head), F32))
        operands = [*feature_parts, by_pairs(w_mine), by_pairs(w_theirs), by_pairs(returned), by_pairs(swapped)]
        operands += [q, low, key_scaled, aux, live]
        return pl.pallas_call(
            functools.partial(half_kernel, heads),
            out_shape=out,
            grid_spec=pltpu.PrefetchScalarGridSpec(
                num_scalar_prefetch=1,
                grid=(1,),
                in_specs=[VM] * heads + [w_spec] * 2 + [c_spec] * 2 + [VM] * 5 + [pl.BlockSpec(memory_space=pl.ANY)] * len(previous),
                out_specs=tuple(pl.BlockSpec((o.shape[0], head // 2), out_map) for o in out),
                scratch_shapes=[
                    pltpu.VMEM((half, 2, rows, head // 2), BF),
                    pltpu.VMEM((2, half // 2, block, LANES), BF),
                ],
            ),
            input_output_aliases={1 + len(operands) + i: i for i in range(len(previous))},
            compiler_params=pltpu.CompilerParams(vmem_limit_bytes=WIDE),
            cost_estimate=pl.CostEstimate(
                flops=window * head * (heads * width + 2 * head + window), bytes_accessed=4 << 20, transcendentals=0
            ),
        )(own, *operands, *previous)

    early = column_half(0, returned, swapped)
    hidden, new_state = column_half(1, weight_near, weight_far, *early)
    return (hidden[None], new_state[None, None], new_norm[None], weight_grad)


def solution(mesh):
    return jax.shard_map(
        on_device,
        mesh=mesh,
        in_specs=(
            P(),
            P("dp"),
            P("dp", None, "mp"),
            P("dp", None, "mp"),
            P("dp", None, "mp"),
            P("dp", None, "mp"),
            P("dp", None, "mp"),
            P("dp", "mp"),
            P("dp", "mp", None, None),
            P("dp", "mp", None),
            P("dp", None, "mp"),
        ),
        out_specs=(
            P("dp", None, "mp"),
            P("dp", "mp", None, None),
            P("dp", "mp", None),
            P("dp", "mp"),
        ),
        check_vma=False,
    )
```

```python
import functools

import functools
import math

import jax
import jax.numpy as jnp
from jax import lax
from jax.experimental import pallas as pl
from jax.experimental.pallas import tpu as pltpu
from jax.sharding import PartitionSpec as P


BF = jnp.bfloat16
F32 = jnp.float32
LANES = 128
WIDE = 56 << 20
VM = pl.BlockSpec(memory_space=pltpu.VMEM)
SM = pl.BlockSpec(memory_space=pltpu.SMEM)


def call(kernel, out, specs, flops, scratch=(), grant=16 << 20):
    moved = sum(o.size * o.dtype.itemsize for o in jax.tree.leaves(out))
    return pl.pallas_call(
        kernel,
        out_shape=out,
        in_specs=specs,
        out_specs=jax.tree.map(lambda _: VM, out),
        scratch_shapes=list(scratch),
        compiler_params=pltpu.CompilerParams(vmem_limit_bytes=grant),
        cost_estimate=pl.CostEstimate(
            flops=flops, bytes_accessed=2 * moved, transcendentals=0
        ),
    )


def shape(dims, dtype):
    return jax.ShapeDtypeStruct(tuple(dims), dtype)


def contract(a, b, da, db):
    return lax.dot_general(
        a, b, (((da,), (db,)), ((), ())), preferred_element_type=F32
    )


def pack_kernel(state_ref, norm_ref, out_ref):
    groups, cols, rows, _ = out_ref.shape
    rows -= 8
    norm = norm_ref[...]
    high = norm.astype(BF)
    low = (norm - high.astype(F32)).astype(BF)
    parts = [p[:, LANES * i : LANES * (i + 1)] for p in (high.astype(F32), low.astype(F32)) for i in range(4)]
    tile = jnp.concatenate(parts, axis=0).astype(BF)
    for i in range(cols):
        block = state_ref[:, LANES * i : LANES * (i + 1)].astype(BF)
        out_ref[:, i, :rows, :] = block.reshape(groups, rows, LANES)
        out_ref[:, i, rows:, :] = jnp.broadcast_to(tile[None], (groups, 8, LANES))


def permute_kernel(map_ref, own_ref, got_ref, w_ref, out_ref, norm_ref):
    half, parts, rows, _ = out_ref.shape
    side = math.isqrt(half)
    tiles = parts - 2
    for k in range(tiles):
        even, odd = (w_ref[:, LANES * i : LANES * (i + 1)] for i in (k, tiles + k))
        for i in range(half):
            tile = odd if (i % 2) ^ (i // side % 2) else even
            out_ref[i, 2 + k] = tile
    own = own_ref[0]

    def body(s, source):
        slot = map_ref[s]
        out_ref[lax.shift_right_logical(slot, 1), slot & 1] = got_ref[s, :rows, :]
        return jnp.where(slot == own, s, source)

    source = lax.fori_loop(0, 2 * half, body, jnp.int32(0), unroll=32)
    tile = got_ref[source, rows:, :].astype(F32)
    total = tile[:4] + tile[4:]
    norm_ref[...] = jnp.concatenate([total[i : i + 1] for i in range(4)], axis=1)


def mix_kernel(own_ref, forget_ref, gate_ref, q_ref, k_ref, low_ref, scaled_ref, aux_ref, tail_ref):
    window = q_ref.shape[0]
    scale = q_ref.shape[1] ** (-0.5)
    length = own_ref[1]
    t = lax.broadcasted_iota(jnp.int32, (window, window), 0)
    s = lax.broadcasted_iota(jnp.int32, (window, window), 1)
    live_row = (lax.broadcasted_iota(jnp.int32, (1, window), 1) < length).astype(F32)
    live_col = (lax.broadcasted_iota(jnp.int32, (window, 1), 0) < length).astype(F32)
    causal = s <= t
    eye = s == t
    forget = forget_ref[...] * live_row
    decay_col = jnp.sum(jnp.where(causal, forget, 0.0), axis=1, keepdims=True)
    decay_row = jnp.sum(jnp.where(eye, decay_col, 0.0), axis=0, keepdims=True)
    weight_row = jnp.exp(gate_ref[...]) * live_row
    mixing = jnp.exp(jnp.where(causal, decay_col - decay_row, -1e30)) * weight_row
    combined = mixing * (contract(q_ref[...], k_ref[...], 1, 1) * scale)
    low_ref[...] = combined.astype(BF)
    inner = jnp.sum(combined, axis=1, keepdims=True)
    last = decay_col[window - 1 :, :]
    tail_row = jnp.exp(last - decay_row) * weight_row * scale
    tail_col = jnp.sum(jnp.where(eye, tail_row, 0.0), axis=1, keepdims=True)
    weighted = k_ref[...].astype(F32) * tail_col
    scaled_ref[...] = weighted.astype(BF)
    tail_ref[...] = jnp.sum(weighted, axis=0, keepdims=True)
    lane = lax.broadcasted_iota(jnp.int32, (window, LANES), 1)
    aux_ref[...] = jnp.where(
        lane == 0, jnp.exp(decay_col), jnp.where(lane == 1, inner, jnp.where(lane == 2, live_col, jnp.exp(last)))
    )


def grad_kernel(norm_ref, q_ref, cot_ref, low_ref, aux_ref, tail_ref, vg_ref, live_ref, new_ref):
    norm = norm_ref[...]
    dot = jnp.sum(q_ref[...].astype(F32) * norm, axis=1, keepdims=True)
    inner = aux_ref[:, 0:1] * dot + aux_ref[:, 1:2]
    live = aux_ref[:, 2:3] / jnp.maximum(jnp.abs(inner), 1.0)
    scaled = (cot_ref[...].astype(F32) * live).astype(BF)
    vg_ref[...] = contract(low_ref[...], scaled, 0, 0).astype(BF)
    live_ref[...] = jnp.broadcast_to(live, live_ref.shape)
    new_ref[...] = aux_ref[0:1, 3:4] * norm + tail_ref[...]


def weight_kernel(own_ref, *refs):
    *f_refs, vg_ref, mine_ref, theirs_ref = refs
    width = f_refs[0].shape[1]
    rows, cols = mine_ref.shape[1:]
    count = width // (2 * rows)
    core = own_ref[2]
    for step, f_ref in enumerate(f_refs):
        part = contract(f_ref[...], vg_ref[...], 0, 0).reshape(count, 2, rows, cols)
        at = pl.ds(count * lax.rem(own_ref[3] + step, len(f_refs)), count)

        @pl.when(core == 0)
        def _():
            mine_ref[at] = part[:, 0]
            theirs_ref[at] = part[:, 1].astype(BF)

        @pl.when(core == 1)
        def _():
            mine_ref[at] = part[:, 1]
            theirs_ref[at] = part[:, 0].astype(BF)


def join_kernel(own_ref, mine_ref, theirs_ref, out_ref):
    side = out_ref.shape[0]
    core = own_ref[2]
    for y in range(side):
        at = slice(side * y, side * (y + 1))
        total = (mine_ref[at] + theirs_ref[at].astype(F32)).astype(BF)

        @pl.when(core == 0)
        def _():
            out_ref[y] = total

        @pl.when(core == 1)
        def _():
            out_ref[:, y] = total


def part_kernel(got_ref, part_ref):
    part_ref[...] = jnp.sum(got_ref[...].astype(F32), axis=0).astype(part_ref.dtype)


def half_kernel(heads, own_ref, *refs):
    f_refs = refs[:heads]
    w_mine_ref, w_theirs_ref, mine_ref, theirs_ref, q_ref, low_ref, scaled_ref, aux_ref, live_ref = refs[heads : heads + 9]
    hidden_ref, new_ref, w_ref, c_ref = refs[-4:]
    width = f_refs[0].shape[1]
    half, _, rows, cols = w_ref.shape
    count = width // (2 * rows)
    core = own_ref[2]
    for i in range(cols // LANES):
        at = slice(LANES * i, LANES * (i + 1))
        w_ref[:, core, :, at] = w_mine_ref[:, :, i].reshape(half, rows, LANES)
        w_ref[:, 1 - core, :, at] = w_theirs_ref[:, :, i].reshape(half, rows, LANES)
    c_ref[core] = mine_ref[:, 0, 0]
    c_ref[1 - core] = theirs_ref[:, 0, 0]
    memory = jnp.concatenate([c_ref[i].reshape(-1, LANES) for i in range(2)], axis=1)
    total = None
    for step, f_ref in enumerate(f_refs):
        at = pl.ds(count * lax.rem(own_ref[3] + step, heads), count)
        part = contract(f_ref[...], w_ref[at].reshape(width, cols), 1, 0)
        total = part if total is None else total + part
    values = total.astype(BF)
    numer = aux_ref[:, 0:1] * contract(q_ref[...], memory, 1, 0) + contract(low_ref[...], values, 1, 0)
    hidden_ref[...] = (numer * live_ref[:, 0:1]).astype(BF)
    new_ref[...] = aux_ref[0:1, 3:4] * memory.astype(F32) + contract(scaled_ref[...], values, 0, 0)


def on_device(
    stream_map,
    lengths,
    features,
    query_rows,
    key_rows,
    log_forget,
    in_gate,
    value_weight,
    state,
    norm_state,
    cotangent,
):
    slots = lax.axis_size("dp")
    heads = lax.axis_size("mp")
    half = slots // 2
    window, head = query_rows.shape[1:]
    width = features.shape[2]
    rows = value_weight.shape[0]
    block = head * head // (slots * LANES)
    lane_groups = head // LANES
    groups = slots // lane_groups
    pairs = [(i, i ^ 1) for i in range(slots)]
    same_core = [list(range(c, slots, 2)) for c in range(2)]
    side = math.isqrt(half)
    along_y = [[[2 * (side * y + z) + c for y in range(side)] for z in range(side)] for c in range(2)]
    along_z = [[[2 * (side * y + z) + c for z in range(side)] for y in range(side)] for c in range(2)]
    every = [(y, z, c) for y in range(side) for z in range(side) for c in range(2)]
    near = [(2 * (side * y + z) + c, 2 * (side * (y ^ c) + (z ^ (1 - c))) + c) for y, z, c in every]
    first, second = along_y[0] + along_z[1], along_z[0] + along_y[1]
    q, k, cot = query_rows[0], key_rows[0], cotangent[0]
    here = lax.axis_index("dp").astype(jnp.int32)
    head_here = lax.axis_index("mp").astype(jnp.int32)
    core = here & 1
    bits = side.bit_length() - 1
    odd_z, odd_y = lax.shift_right_logical(here, 1) & 1, lax.shift_right_logical(here, 1 + bits) & 1
    own = jnp.stack([here, lengths[0], core, head_here, odd_y ^ odd_z])

    def exchange(x, index_groups=None):
        return lax.all_to_all(x, "dp", 0, 0, axis_index_groups=index_groups, tiled=True)

    packed = call(
        pack_kernel, shape((groups, lane_groups, block + 8, LANES), BF), [VM, VM], 10**6, grant=WIDE
    )(state[0, 0], norm_state[0]).reshape(slots, block + 8, LANES)
    spread = exchange(packed)
    feature_parts = [features[0]] + [
        lax.ppermute(features[0], "mp", [((j + step) % heads, j) for j in range(heads)])
        for step in range(1, heads)
    ]

    low, key_scaled, aux, tail = call(
        mix_kernel,
        (
            shape((window, window), BF),
            shape((window, head), BF),
            shape((window, LANES), F32),
            shape((1, head), F32),
        ),
        [SM, VM, VM, VM, VM],
        2 * window * window * head,
    )(own, log_forget[0].reshape(1, window), in_gate[0].reshape(1, window), q, k)

    picked, norm = call(
        permute_kernel,
        (shape((half, 2 + lane_groups // 2, block, LANES), BF), shape((1, head), F32)),
        [SM, SM, VM, VM],
        10**6,
    )(stream_map, own, spread, value_weight)
    returned = exchange(picked, same_core)

    value_grad, live, new_norm = call(
        grad_kernel,
        (shape((window, head), BF), shape((window, LANES), F32), shape((1, head), F32)),
        [VM] * 6,
        2 * window * window * head,
    )(norm, q, cot, low, aux, tail)
    mine, theirs = call(
        weight_kernel,
        (shape((half, rows, head), F32), shape((half, rows, head), BF)),
        [SM] + [VM] * (heads + 1),
        2 * window * heads * width * head,
    )(own, *feature_parts, value_grad)
    joined = call(join_kernel, shape((side, side, rows, head), BF), [SM, VM, VM], 10**6)(
        own, mine, lax.ppermute(theirs, "dp", pairs)
    )
    part = call(part_kernel, shape((side, rows, head), BF), [VM], 10**6)(exchange(joined, first))
    weight_grad = call(part_kernel, shape((rows, head), F32), [VM], 10**5)(exchange(part, second))
    weight_near = lax.ppermute(returned[:, 2:], "dp", near)
    swapped = lax.ppermute(returned, "dp", pairs)
    weight_far = lax.ppermute(weight_near, "dp", pairs)

    def by_pairs(x):
        return x.reshape(half // 2, 2, *x.shape[1:])

    def column_half(flip, w_mine, w_theirs, *previous):
        def out_map(i, own):
            return 0, own[4] ^ flip

        tiles = lane_groups // 2
        at_part = w_mine.shape[1] // tiles - 1
        w_spec = pl.BlockSpec((half // 2, 2, tiles, block, LANES), lambda i, own: (0, 0, at_part, 0, 0))
        c_spec = pl.BlockSpec(
            (half // 2, 1, 1, block, LANES), lambda i, own: (0, own[4] ^ flip, own[2], 0, 0)
        )
        out = (shape((window, head), BF), shape((head, head), F32))
        operands = [*feature_parts, by_pairs(w_mine), by_pairs(w_theirs), by_pairs(returned), by_pairs(swapped)]
        operands += [q, low, key_scaled, aux, live]
        return pl.pallas_call(
            functools.partial(half_kernel, heads),
            out_shape=out,
            grid_spec=pltpu.PrefetchScalarGridSpec(
                num_scalar_prefetch=1,
                grid=(1,),
                in_specs=[VM] * heads + [w_spec] * 2 + [c_spec] * 2 + [VM] * 5 + [pl.BlockSpec(memory_space=pl.ANY)] * len(previous),
                out_specs=tuple(pl.BlockSpec((o.shape[0], head // 2), out_map) for o in out),
                scratch_shapes=[
                    pltpu.VMEM((half, 2, rows, head // 2), BF),
                    pltpu.VMEM((2, half // 2, block, LANES), BF),
                ],
            ),
            input_output_aliases={1 + len(operands) + i: i for i in range(len(previous))},
            compiler_params=pltpu.CompilerParams(vmem_limit_bytes=WIDE),
            cost_estimate=pl.CostEstimate(
                flops=window * head * (heads * width + 2 * head + window), bytes_accessed=4 << 20, transcendentals=0
            ),
        )(own, *operands, *previous)

    early = column_half(0, returned, swapped)
    hidden, new_state = column_half(1, weight_near, weight_far, *early)
    return (hidden[None], new_state[None, None], new_norm[None], weight_grad)


def solution(mesh):
    return jax.shard_map(
        on_device,
        mesh=mesh,
        in_specs=(
            P(),
            P("dp"),
            P("dp", None, "mp"),
            P("dp", None, "mp"),
            P("dp", None, "mp"),
            P("dp", None, "mp"),
            P("dp", None, "mp"),
            P("dp", "mp"),
            P("dp", "mp", None, None),
            P("dp", "mp", None),
            P("dp", None, "mp"),
        ),
        out_specs=(
            P("dp", None, "mp"),
            P("dp", "mp", None, None),
            P("dp", "mp", None),
            P("dp", "mp"),
        ),
        check_vma=False,
    )
```
